32 devices in a mesh: ctx: 4 (over y, core), exp: 8 (over z, x).
Axes of the slice: x: 2, y: 2, z: 4, core: 2. Of those that a mesh axis runs over, the one named last changes fastest.
Arguments:
- stream: bfloat16 [8, 512, 2048], P('exp', 'ctx'), may hold values from -16 to 16
- queries: bfloat16 [8, 512, 1024], P('exp', 'ctx'), may hold values from -6 to 6
- key_proj: bfloat16 [8, 512, 1024], P('exp', 'ctx'), may hold values from -6 to 6
- value_proj: bfloat16 [8, 512, 2048], P('exp', 'ctx'), may hold values from -6 to 6
- gate_proj: bfloat16 [8, 512, 2048], P('exp', 'ctx'), may hold values from -6 to 6
- write_rate: float32 [8, 512, 16], P('exp', 'ctx'), may hold values from 0.02 to 0.3
- log_decay: float32 [8, 512, 16], P('exp', 'ctx'), may hold values from -1 to 0
- init_state: float32 [8, 16, 128, 128], P('exp'), may hold values from -0.6 to 0.6
- head_gain: float32 [128], replicated, may hold values from 0.1 to 1.9
- out_weight: bfloat16 [2048, 2048], P(None, 'ctx'), may hold values from -0.125 to 0.125
- moe_gain: float32 [2048], replicated, may hold values from 0.1 to 1.9
- routes: int32 [8, 512, 10], P('exp', 'ctx'), may hold values from 0 to 31, as said below
- route_gate: float32 [8, 512, 10], P('exp', 'ctx'), may hold values from 0.05 to 0.2
- expert_up: bfloat16 [32, 2048, 1024], P(('ctx', 'exp')), may hold values from -0.125 to 0.125
- expert_down: bfloat16 [32, 512, 2048], P(('ctx', 'exp')), may hold values from -0.25 to 0.25
Outputs:
- mixed: bfloat16 [8, 512, 2048], P('exp', 'ctx')
- moe_output: bfloat16 [8, 512, 2048], P('exp', 'ctx')
The draws below stay inside these ranges and needn't reach their ends.
Inputs may be any that keep to these rules, and one draw needn't show every extreme that they name: `routes`: within the 128 tokens of one device the 10 ids of a token differ, and every expert id is named exactly 128 * 10 / 32 times.
All inputs are finite; a program needn't handle non-finite values.
Results may differ from the reference program's by a relative error of at most 0.019.
Values may be sent and summed in bfloat16 or wider, within the bound.
A program may use at most 128 MiB of HBM per device.

```python
import jax
import jax.numpy as jnp
from jax import lax

D = 2048
HK = 8
OUTPUT_CHANNELS = 16
DK = 128
DV = 128
FF = 512
TOP = 10
TOK_DEV = 128
EXPERTS = 32
BATCH_SAMPLES = 8
SPAN_ITEMS = 512


def draw_stream(key, part):
    shape = (BATCH_SAMPLES, SPAN_ITEMS, D)
    key_a = jax.random.fold_in(jax.random.fold_in(key, 11), 0)
    return jax.random.truncated_normal(key_a, -6.0, 6.0, shape, jnp.float32).astype(jnp.bfloat16)


def draw_log_decay(key, part):
    blocks = SPAN_ITEMS // TOK_DEV
    lookup_matrix = jax.random.split(jax.random.fold_in(key, 23), 7)
    share = 0.5
    fast = jax.random.bernoulli(lookup_matrix[0], share, (BATCH_SAMPLES, 1, OUTPUT_CHANNELS))
    slow_rate = jnp.exp(jax.random.uniform(lookup_matrix[1], (BATCH_SAMPLES, 1, OUTPUT_CHANNELS), jnp.float32, jnp.log(0.05), jnp.log(0.6))) / SPAN_ITEMS
    fast_rate = 1.0 / jax.random.uniform(lookup_matrix[2], (BATCH_SAMPLES, 1, OUTPUT_CHANNELS), jnp.float32, 30.0, 50.0)
    forget_gate = jnp.where(fast, fast_rate, slow_rate)
    segment_factor = jnp.exp(jax.random.uniform(lookup_matrix[3], (BATCH_SAMPLES, blocks, 1, OUTPUT_CHANNELS), jnp.float32, jnp.log(0.5), jnp.log(2.0)))
    segment_factor = jnp.broadcast_to(segment_factor, (BATCH_SAMPLES, blocks, TOK_DEV, OUTPUT_CHANNELS)).reshape(BATCH_SAMPLES, SPAN_ITEMS, OUTPUT_CHANNELS)
    element_factor = jax.random.uniform(lookup_matrix[4], (BATCH_SAMPLES, SPAN_ITEMS, OUTPUT_CHANNELS), jnp.float32, 0.5, 1.5)
    segment_offset = jax.random.bernoulli(lookup_matrix[5], 3.0 / SPAN_ITEMS, (BATCH_SAMPLES, SPAN_ITEMS, OUTPUT_CHANNELS))
    segment_size = -jnp.log(1.0 - jax.random.uniform(lookup_matrix[6], (BATCH_SAMPLES, SPAN_ITEMS, OUTPUT_CHANNELS), jnp.float32, 0.2, 0.5))
    return -(forget_gate * segment_factor * element_factor) - jnp.where(segment_offset, segment_size, 0.0)


def draw_routes(key, part):
    blocks = BATCH_SAMPLES * SPAN_ITEMS // TOK_DEV
    lookup_matrix = jax.random.split(jax.random.fold_in(key, 37), blocks)
    slots = (jnp.arange(TOK_DEV, dtype=jnp.int32)[:, None] * TOP + jnp.arange(TOP, dtype=jnp.int32)[None, :]) % EXPERTS

    def one_block(block_key):
        key_a, key_b = jax.random.split(block_key)
        relabel = jax.random.permutation(key_a, EXPERTS).astype(jnp.int32)
        shuffle = jax.random.permutation(key_b, TOK_DEV).astype(jnp.int32)
        return relabel[slots][shuffle]
    return jax.vmap(one_block)(lookup_matrix).reshape(BATCH_SAMPLES, SPAN_ITEMS, TOP).astype(jnp.int32)


def block_scale(key, dims, cuts, smallest, top_value):
    level = 1.0
    for axis_at, blocks in cuts:
        steps = jax.random.uniform(jax.random.fold_in(jax.random.fold_in(key, 6), axis_at), (blocks,), jnp.float32, smallest / len(cuts), top_value / len(cuts))
        level = level * jnp.repeat(jnp.exp(steps), dims[axis_at] // blocks).reshape((-1,) + (1,) * (len(dims) - 1 - axis_at))
    return level


def normal_values(stream_key, extent, spread, most, cuts=(), kind=jnp.bfloat16):
    factor_of = block_scale(stream_key, extent, cuts, -0.22, 0.18) if cuts else 1.0
    array = jax.random.normal(stream_key, extent, jnp.float32) * spread * factor_of
    return jnp.minimum(jnp.maximum(array, -most), most).astype(kind)


def setup_inputs(seed: int = 0) -> dict:
    arg_keys = jax.random.split(jax.random.key(seed), 16)
    stream = draw_stream(jax.random.fold_in(arg_keys[15], 71), 0)
    queries = normal_values(arg_keys[1], (BATCH_SAMPLES, SPAN_ITEMS, HK * DK), 1.0, 6.0, ((0, 8), (1, 4)))
    key_proj = normal_values(arg_keys[2], (BATCH_SAMPLES, SPAN_ITEMS, HK * DK), 1.0, 6.0, ((0, 8), (1, 4)))
    value_proj = normal_values(arg_keys[3], (BATCH_SAMPLES, SPAN_ITEMS, OUTPUT_CHANNELS * DV), 1.0, 6.0, ((0, 8), (1, 4)))
    gate_proj = normal_values(arg_keys[4], (BATCH_SAMPLES, SPAN_ITEMS, OUTPUT_CHANNELS * DV), 1.0, 6.0, ((0, 8), (1, 4)))
    write_rate = jnp.clip(0.02 + 0.28 * jax.random.uniform(arg_keys[5], (BATCH_SAMPLES, SPAN_ITEMS, OUTPUT_CHANNELS), jnp.float32) ** block_scale(arg_keys[5], (BATCH_SAMPLES, SPAN_ITEMS, OUTPUT_CHANNELS), ((0, 8), (1, 4)), -0.2, 0.2), 0.02, 0.3)
    log_decay = draw_log_decay(jax.random.fold_in(arg_keys[15], 71), 0)
    init_state = normal_values(arg_keys[7], (BATCH_SAMPLES, OUTPUT_CHANNELS, DK, DV), 0.1, 0.6, ((0, 8),), jnp.float32)
    head_gain = jnp.clip(1.0 + 0.18 * jax.random.normal(arg_keys[8], (DV,), jnp.float32), 0.1, 1.9)
    out_weight = normal_values(arg_keys[9], (OUTPUT_CHANNELS * DV, D), (OUTPUT_CHANNELS * DV) ** -0.5, 0.125, ((1, 4),))
    moe_gain = jnp.clip(1.0 + 0.18 * jax.random.normal(arg_keys[10], (D,), jnp.float32), 0.1, 1.9)
    routes = draw_routes(jax.random.fold_in(arg_keys[15], 71), 0)
    route_gate = jnp.clip(0.05 + 0.15 * jax.random.uniform(arg_keys[12], (BATCH_SAMPLES, SPAN_ITEMS, TOP), jnp.float32) ** block_scale(arg_keys[12], (BATCH_SAMPLES, SPAN_ITEMS, TOP), ((0, 8), (1, 4)), -0.2, 0.2), 0.05, 0.2)
    expert_up = normal_values(arg_keys[13], (EXPERTS, D, 2 * FF), D ** -0.5, 0.125, ((0, 32),))
    expert_down = normal_values(arg_keys[14], (EXPERTS, FF, D), FF ** -0.5, 0.25, ((0, 32),))
    return dict(stream=stream, queries=queries, key_proj=key_proj, value_proj=value_proj, gate_proj=gate_proj, write_rate=write_rate, log_decay=log_decay, init_state=init_state, head_gain=head_gain, out_weight=out_weight, moe_gain=moe_gain, routes=routes, route_gate=route_gate, expert_up=expert_up, expert_down=expert_down)


def reference(stream, queries, key_proj, value_proj, gate_proj, write_rate, log_decay, init_state, head_gain, out_weight, moe_gain, routes, route_gate, expert_up, expert_down):
    highest = lax.Precision.HIGHEST
    repeat = OUTPUT_CHANNELS // HK
    query_all = queries.astype(jnp.float32).reshape(BATCH_SAMPLES, SPAN_ITEMS, HK, DK)
    key_all = key_proj.astype(jnp.float32).reshape(BATCH_SAMPLES, SPAN_ITEMS, HK, DK)
    key_all = key_all * lax.rsqrt(lax.optimization_barrier(jnp.sum(key_all * key_all, axis=-1, keepdims=True)) + 1e-06)
    value_all = value_proj.astype(jnp.float32).reshape(BATCH_SAMPLES, SPAN_ITEMS, OUTPUT_CHANNELS, DV)

    def advance(state, inputs):
        query_now, key_now, value_now, rate_now, decay_now = inputs
        query_now = jnp.repeat(query_now, repeat, axis=1)
        key_now = jnp.repeat(key_now, repeat, axis=1)
        state = jnp.exp(decay_now)[:, :, None, None] * state
        predicted = jnp.einsum('shkv,shk->shv', state, key_now, precision=highest)
        state = state + rate_now[:, :, None, None] * key_now[:, :, :, None] * (value_now - predicted)[:, :, None, :]
        emitted = jnp.einsum('shkv,shk->shv', state, query_now, precision=highest)
        return (state, emitted)
    inputs = (jnp.moveaxis(query_all, 1, 0), jnp.moveaxis(key_all, 1, 0), jnp.moveaxis(value_all, 1, 0), jnp.moveaxis(write_rate.astype(jnp.float32), 1, 0), jnp.moveaxis(log_decay.astype(jnp.float32), 1, 0))
    _, emitted = lax.scan(advance, init_state.astype(jnp.float32), inputs)
    head_out = jnp.moveaxis(emitted, 0, 1)
    gate_all = gate_proj.astype(jnp.float32).reshape(BATCH_SAMPLES, SPAN_ITEMS, OUTPUT_CHANNELS, DV)
    square_mean = lax.optimization_barrier(jnp.mean(head_out * head_out, axis=-1, keepdims=True))
    gated = (head_out * lax.rsqrt(square_mean + 1e-06) * head_gain * jax.nn.silu(gate_all)).astype(jnp.bfloat16)
    gated = gated.reshape(BATCH_SAMPLES * SPAN_ITEMS, OUTPUT_CHANNELS * DV)
    attn = jnp.dot(gated, out_weight, preferred_element_type=jnp.float32)
    mixed = (stream.reshape(BATCH_SAMPLES * SPAN_ITEMS, D).astype(jnp.float32) + attn).astype(jnp.bfloat16)
    mixed_f = mixed.astype(jnp.float32)
    moe_in = (mixed_f * lax.rsqrt(lax.optimization_barrier(jnp.mean(mixed_f * mixed_f, axis=-1, keepdims=True)) + 1e-06) * moe_gain).astype(jnp.bfloat16)
    flat_routes = routes.reshape(-1).astype(jnp.int32)
    flat_gates = route_gate.reshape(-1).astype(jnp.float32)
    per_expert = BATCH_SAMPLES * SPAN_ITEMS * TOP // EXPERTS
    order_all = jnp.argsort(flat_routes, stable=True).astype(jnp.int32).reshape(EXPERTS, per_expert)

    def one_expert(total, inputs):
        up_now, down_now, picked = inputs
        token_ids = picked // TOP
        rows = moe_in[token_ids]
        pre = jnp.dot(rows, up_now, preferred_element_type=jnp.float32)
        hidden = (jax.nn.silu(pre[:, :FF]) * pre[:, FF:]).astype(jnp.bfloat16)
        produced = jnp.dot(hidden, down_now, preferred_element_type=jnp.float32).astype(jnp.bfloat16)
        total = total.at[token_ids].add(flat_gates[picked][:, None] * produced.astype(jnp.float32))
        return (total, None)
    total, _ = lax.scan(one_expert, jnp.zeros((BATCH_SAMPLES * SPAN_ITEMS, D), jnp.float32), (expert_up, expert_down, order_all))
    moe_output = total.astype(jnp.bfloat16).reshape(BATCH_SAMPLES, SPAN_ITEMS, D)
    return (mixed.reshape(BATCH_SAMPLES, SPAN_ITEMS, D), moe_output)
```

```python
import functools

import jax
import jax.numpy as jnp
from jax import lax
from jax.experimental import pallas as pl
from jax.experimental.pallas import tpu as pltpu
from jax.sharding import PartitionSpec as P

D = 2048
HK = 8
OUTPUT_CHANNELS = 16
DK = 128
DV = 128
FF = 512
TOP = 10


def shifted(value, axis, steps):
    count = lax.axis_size(axis)
    first, last = (max(0, -steps), min(count, count - steps))
    return lax.ppermute(value, axis, [(source, source + steps) for source in range(first, last)])


BF = jnp.bfloat16
MESH = pl.DeviceIdType.MESH
BASE = 16


def mm(a, b):
    return lax.dot_general(
        a.astype(BF), b.astype(BF), (((1,), (0,)), ((), ())), preferred_element_type=jnp.float32
    )


def mm_nt(a, b):
    return lax.dot_general(
        a.astype(BF), b.astype(BF), (((1,), (1,)), ((), ())), preferred_element_type=jnp.float32
    )


def mm_tn(a, b):
    return lax.dot_general(
        a.astype(BF), b.astype(BF), (((0,), (0,)), ((), ())), preferred_element_type=jnp.float32
    )


def unit_lower_inverse(lowers, rows, cols, eye):
    length = rows.shape[0]
    same = (rows // BASE) == (cols // BASE)
    powers = [jnp.where(same, -low, 0.0) for low in lowers]
    xs = [eye + p for p in powers]
    span = 2
    while span < BASE:
        powers = [mm(p, p) for p in powers]
        xs = [x + mm(x, p) for x, p in zip(xs, powers)]
        span *= 2
    size = BASE
    while size < length:
        inside = ((rows // (2 * size)) == (cols // (2 * size))) & ((rows // size) > (cols // size))
        mids = [mm(jnp.where(inside, low, 0.0), x) for low, x in zip(lowers, xs)]
        xs = [x - mm(x, m) for x, m in zip(xs, mids)]
        size *= 2
    return xs


def delta_head(query, keys, values, rate_rows, cum_rows):
    length = query.shape[0]
    rows = lax.broadcasted_iota(jnp.int32, (length, length), 0)
    cols = lax.broadcasted_iota(jnp.int32, (length, length), 1)
    diag = rows == cols
    eye = jnp.where(diag, 1.0, 0.0)
    query = query.astype(jnp.float32)
    key = keys.astype(jnp.float32)
    key = key * lax.rsqrt(jnp.sum(key * key, axis=-1, keepdims=True) + 1e-06)
    kk = mm_nt(key, key)
    qk = mm_nt(query, key)
    column = lambda row: jnp.sum(jnp.where(diag, row, 0.0), axis=1, keepdims=True)
    lowers, parts = [], []
    for value, rate_row, cum_row in zip(values, rate_rows, cum_rows):
        cum, rate = column(cum_row), column(rate_row)
        last = cum_row[:, length - 1 :]
        spread = jnp.exp(jnp.where(rows >= cols, cum - cum_row, 0.0))
        lowers.append(jnp.where(rows > cols, rate * spread * kk, 0.0))
        parts.append((value.astype(jnp.float32), cum, rate, last, spread))
    inverses = unit_lower_inverse(lowers, rows, cols, eye)
    results = []
    for inverse, (value, cum, rate, last, spread) in zip(inverses, parts):
        now = jnp.exp(cum)
        solved = mm(inverse, jnp.concatenate([rate * value, (rate * now) * key], axis=1))
        attend = jnp.where(rows >= cols, spread * qk, 0.0)
        inner = mm(attend, solved)
        tail = mm_tn(jnp.exp(last - cum) * key, solved)
        dv = value.shape[1]
        results.append(
            (
                inner[:, :dv],
                now * query - inner[:, dv:],
                jnp.exp(last) * eye - tail[:, dv:],
                tail[:, :dv],
            )
        )
    return results


def delta_kernel(group, q_ref, k_ref, v_ref, rate_ref, cum_ref, intra_ref, qeff_ref, trans_ref, add_ref):
    width = v_ref.shape[1] // group
    results = delta_head(
        q_ref[...],
        k_ref[...],
        [v_ref[:, i * width : (i + 1) * width] for i in range(group)],
        [rate_ref[0, i : i + 1, :] for i in range(group)],
        [cum_ref[0, i : i + 1, :] for i in range(group)],
    )
    for i, (intra, qeff, trans, add) in enumerate(results):
        intra_ref[i] = intra
        qeff_ref[i] = qeff.astype(qeff_ref.dtype)
        trans_ref[i] = trans
        add_ref[i] = add


def delta_local(query, key, value, rate, cum):
    length = query.shape[0]
    heads = rate.shape[0]
    group = heads // HK
    out = jax.ShapeDtypeStruct((heads, length, DV), jnp.float32)
    outb = jax.ShapeDtypeStruct((heads, length, DK), BF)
    sq = jax.ShapeDtypeStruct((heads, DK, DK), jnp.float32)
    sv = jax.ShapeDtypeStruct((heads, DK, DV), jnp.float32)
    block = lambda a, b: pl.BlockSpec((group, a, b), lambda h: (h, 0, 0))
    rows = pl.BlockSpec((1, group, length), lambda h: (h, 0, 0))
    return pl.pallas_call(
        functools.partial(delta_kernel, group),
        out_shape=(out, outb, sq, sv),
        grid=(HK,),
        in_specs=[
            pl.BlockSpec((length, DK), lambda h: (0, h)),
            pl.BlockSpec((length, DK), lambda h: (0, h)),
            pl.BlockSpec((length, group * DV), lambda h: (0, h)),
            rows,
            rows,
        ],
        out_specs=(block(length, DV), block(length, DK), block(DK, DK), block(DK, DV)),
        cost_estimate=pl.CostEstimate(flops=20 * heads * 2 * length**3, bytes_accessed=8 << 20, transcendentals=heads * length * length),
    )(query, key, value, rate.reshape(HK, group, length), cum.reshape(HK, group, length))


def moe_kernel(
    planes, lanes_x, tok_ref, pick_ref, up_ref, down_ref, out_ref,
    tokbuf, pickbuf, sendbuf, recvbuf, prodbuf, retbuf, partbuf, zbuf, total,
    tok_send, tok_recv, pick_send, pick_recv, d_send, d_recv, r_send, r_recv, z_send, z_recv,
):
    c = lax.axis_index("ctx")
    e = lax.axis_index("exp")
    z = e // lanes_x
    x = e % lanes_x
    ctx = lax.axis_size("ctx")
    peers = ctx * lanes_x
    mine = c * lanes_x + x
    slots = sendbuf.shape[2]
    width = tok_ref.shape[1]
    ff = down_ref.shape[0]

    def plane_device(q):
        return (q // lanes_x, z * lanes_x + q % lanes_x)

    def line_device(zz):
        return (c, zz * lanes_x + x)

    barrier = pltpu.get_barrier_semaphore()
    for d in range(1, peers):
        pl.semaphore_signal(barrier, inc=1, device_id=plane_device((mine + d) % peers), device_id_type=MESH)
    for d in range(1, planes):
        pl.semaphore_signal(barrier, inc=1, device_id=line_device((z + d) % planes), device_id_type=MESH)
    pl.semaphore_wait(barrier, peers + planes - 2)

    def remote(src, dst, ssem, rsem, device):
        return pltpu.make_async_remote_copy(
            src_ref=src, dst_ref=dst, send_sem=ssem, recv_sem=rsem, device_id=device, device_id_type=MESH
        )

    def step_of(i):
        return (i % 2) * ((i + 1) // 2) + (1 - i % 2) * ((planes - i // 2) % planes)

    def tok_copy(s):
        return remote(tok_ref, tokbuf.at[s], tok_send.at[s], tok_recv.at[s], line_device((z + s) % planes))

    def pick_copy(s):
        there = (z + s) % planes
        return remote(pick_ref.at[there], pickbuf.at[s], pick_send.at[s], pick_recv.at[s], line_device(there))

    def d_copy(s, q):
        return remote(sendbuf.at[s, q], recvbuf.at[s, mine], d_send.at[s, q], d_recv.at[s, mine], plane_device(q))

    def d_arrival(s, q):
        return remote(sendbuf.at[s, q], recvbuf.at[s, q], d_send.at[s, q], d_recv.at[s, q], plane_device(q))

    def r_copy(s, q):
        return remote(prodbuf.at[s, q], retbuf.at[s, mine], r_send.at[s, q], r_recv.at[s, mine], plane_device(q))

    def r_arrival(s, q):
        return remote(prodbuf.at[s, q], retbuf.at[s, q], r_send.at[s, q], r_recv.at[s, q], plane_device(q))

    def z_copy(s):
        return remote(partbuf.at[s], zbuf.at[s], z_send.at[s], z_recv.at[s], line_device((z - s + planes) % planes))

    for i in range(1, planes):
        s = (i + 1) // 2 if i % 2 else (planes - i // 2) % planes
        pick_copy(s).start()
        tok_copy(s).start()
    tokbuf[0] = tok_ref[...]
    pickbuf[0] = pick_ref[z]

    def body(i, carry):
        @pl.when(i < planes)
        def _():
            s = step_of(i)

            @pl.when(i > 0)
            def _():
                pick_copy(s).wait_recv()
                tok_copy(s).wait_recv()

            chosen = jnp.where(pickbuf[s].astype(jnp.float32) != 0.0, 1.0, 0.0).astype(BF)
            rows = mm(chosen, tokbuf[s])
            sendbuf[s] = rows.reshape(peers, slots, width).astype(BF)
            for d in range(1, peers):
                d_copy(s, (mine + d) % peers).start()
            recvbuf[s, mine] = sendbuf[s, mine]

        @pl.when((i >= 1) & (i < planes + 1))
        def _():
            s = step_of(i - 1)
            for d in range(1, peers):
                d_arrival(s, (mine + d) % peers).wait_recv()
            rows = recvbuf[s].astype(jnp.float32).reshape(peers * slots, width).astype(BF)
            gate = mm(rows, up_ref[:, :ff])
            hidden = (gate / (1.0 + jnp.exp(-gate)) * mm(rows, up_ref[:, ff:])).astype(BF)
            made = mm(hidden, down_ref[...])
            prodbuf[s] = made.reshape(peers, slots, width).astype(BF)
            for d in range(1, peers):
                r_copy(s, (mine + d) % peers).start()
            retbuf[s, mine] = prodbuf[s, mine]

        @pl.when(i >= 2)
        def _():
            s = step_of(i - 2)
            for d in range(1, peers):
                r_arrival(s, (mine + d) % peers).wait_recv()
            rows = retbuf[s].astype(jnp.float32).reshape(peers * slots, width).astype(BF)
            part = mm_tn(pickbuf[s], rows)

            @pl.when(i == 2)
            def _():
                total[...] = part

            @pl.when(i > 2)
            def _():
                partbuf[s] = part.astype(BF)
                z_copy(s).start()

        return carry

    lax.fori_loop(0, planes + 2, body, 0)

    for s in range(1, planes):
        z_copy(s).wait_recv()
        total[...] += zbuf[s].astype(jnp.float32)
    out_ref[...] = total[...].astype(out_ref.dtype)

    for s in range(1, planes):
        tok_copy(s).wait_send()
        pick_copy(s).wait_send()
        z_copy(s).wait_send()

    def drain(s, carry):
        for d in range(1, peers):
            d_copy(s, (mine + d) % peers).wait_send()
            r_copy(s, (mine + d) % peers).wait_send()
        return carry

    lax.fori_loop(0, planes, drain, 0)


def moe_planes(moe_in, routes, route_gate, expert_up, expert_down, planes, lanes_x):
    length, width = moe_in.shape
    ctx = lax.axis_size("ctx")
    peers = ctx * lanes_x
    experts = peers * planes
    slots = length * TOP // experts
    ids = jnp.arange(experts, dtype=jnp.int32)
    hit = routes[:, :, None] == ids
    named = jnp.any(hit, axis=1)
    weight = jnp.sum(jnp.where(hit, route_gate[:, :, None], 0.0), axis=1).T
    ones = named.astype(BF)
    before = (
        lax.broadcasted_iota(jnp.int32, (length, length), 0)
        < lax.broadcasted_iota(jnp.int32, (length, length), 1)
    ).astype(BF)
    rank = lax.dot_general(ones, before, (((0,), (0,)), ((), ())), preferred_element_type=jnp.float32)
    rank = jnp.where(named.T, rank, -1.0)

    def by_plane(v):
        return v.reshape(ctx, planes, lanes_x, length).transpose(1, 0, 2, 3)

    slot = jnp.arange(slots, dtype=jnp.float32)[None, None, None, :, None]
    pick = jnp.where(by_plane(rank)[:, :, :, None, :] == slot, by_plane(weight)[:, :, :, None, :], 0.0)
    pick = pick.astype(BF).reshape(planes, peers * slots, length)
    dma = pltpu.SemaphoreType.DMA
    rows_shape = pltpu.VMEM((planes, peers, slots, width), BF)
    block = pltpu.VMEM((planes, length, width), BF)
    return pl.pallas_call(
        functools.partial(moe_kernel, planes, lanes_x),
        out_shape=jax.ShapeDtypeStruct((length, width), BF),
        in_specs=[pl.BlockSpec(memory_space=pltpu.VMEM)] * 4,
        out_specs=pl.BlockSpec(memory_space=pltpu.VMEM),
        scratch_shapes=[
            block,
            pltpu.VMEM((planes, peers * slots, length), BF),
            rows_shape, rows_shape, rows_shape, rows_shape,
            block,
            block,
            pltpu.VMEM((length, width), jnp.float32),
            dma((planes,)), dma((planes,)), dma((planes,)), dma((planes,)),
            dma((planes, peers)), dma((planes, peers)), dma((planes, peers)), dma((planes, peers)),
            dma((planes,)), dma((planes,)),
        ],
        compiler_params=pltpu.CompilerParams(collective_id=1, has_side_effects=True, vmem_limit_bytes=60 << 20),
    )(moe_in, pick, expert_up[0], expert_down[0])


def on_device(
    stream,
    queries,
    key_proj,
    value_proj,
    gate_proj,
    write_rate,
    log_decay,
    init_state,
    head_gain,
    out_weight,
    moe_gain,
    routes,
    route_gate,
    expert_up,
    expert_down,
):
    highest = lax.Precision.HIGHEST
    length = stream.shape[1]
    cumulative = jnp.cumsum(log_decay[0], axis=0).T
    intra, query_eff, transit, carry_add = delta_local(
        queries[0], key_proj[0], value_proj[0], write_rate[0].T, cumulative
    )
    first_state = init_state[0]
    position = lax.axis_index("ctx")

    def relay_step(turn, start_state):
        end_state = jnp.einsum("hde,hev->hdv", transit, start_state, precision=highest) + carry_add
        incoming = shifted(end_state, "ctx", 1)
        return jnp.where(position == 0, first_state, incoming)

    start_state = lax.fori_loop(0, lax.axis_size("ctx") - 1, relay_step, first_state)
    head_out = intra + jnp.einsum(
        "htd,hdv->htv", query_eff, start_state.astype(BF), preferred_element_type=jnp.float32
    )
    gate_loc = (
        gate_proj[0].astype(jnp.float32).reshape(length, OUTPUT_CHANNELS, DV).transpose(1, 0, 2)
    )
    square_mean = jnp.mean(head_out * head_out, axis=-1, keepdims=True)
    gated = head_out * lax.rsqrt(square_mean + 1e-06) * head_gain * jax.nn.silu(gate_loc)
    gated = gated.transpose(1, 0, 2).reshape(length, OUTPUT_CHANNELS * DV).astype(jnp.bfloat16)
    column_block = jnp.dot(
        lax.all_gather(gated, "ctx", axis=0, tiled=True),
        out_weight,
        preferred_element_type=jnp.float32,
    )
    attn = lax.all_to_all(column_block, "ctx", split_axis=0, concat_axis=1, tiled=True)
    mixed = (stream[0].astype(jnp.float32) + attn).astype(jnp.bfloat16)
    mixed_f = mixed.astype(jnp.float32)
    moe_in = (
        mixed_f * lax.rsqrt(jnp.mean(mixed_f * mixed_f, axis=-1, keepdims=True) + 1e-06) * moe_gain
    ).astype(jnp.bfloat16)
    ctx_count = lax.axis_size("ctx")
    exp_count = lax.axis_size("exp")
    local_experts = expert_up.shape[0]
    lanes_x = max(1, ctx_count // 2)
    even = exp_count % lanes_x == 0 and length * TOP % (8 * ctx_count * exp_count) == 0
    if local_experts == 1 and even:
        moe_output = moe_planes(
            moe_in, routes[0], route_gate[0], expert_up, expert_down, exp_count // lanes_x, lanes_x
        )
        return (mixed[None], moe_output[None])
    flat_routes = routes[0].reshape(-1)
    order = jnp.argsort(flat_routes, stable=True)
    per_owner = length * TOP // (ctx_count * exp_count)
    outgoing = moe_in[order // TOP].reshape(ctx_count, exp_count, per_owner, D)
    arrived = lax.all_to_all(
        lax.all_to_all(outgoing, "ctx", split_axis=0, concat_axis=0, tiled=True),
        "exp",
        split_axis=1,
        concat_axis=1,
        tiled=True,
    )
    slot_count = per_owner // local_experts
    grouped = arrived.reshape(ctx_count * exp_count, local_experts, slot_count, D).transpose(
        1, 0, 2, 3
    )
    grouped = grouped.reshape(local_experts, ctx_count * exp_count * slot_count, D)
    pre = jnp.einsum("erd,edf->erf", grouped, expert_up, preferred_element_type=jnp.float32)
    hidden = (jax.nn.silu(pre[:, :, :FF]) * pre[:, :, FF:]).astype(jnp.bfloat16)
    produced = jnp.einsum(
        "erf,efd->erd", hidden, expert_down, preferred_element_type=jnp.float32
    ).astype(jnp.bfloat16)
    produced = produced.reshape(local_experts, ctx_count * exp_count, slot_count, D).transpose(
        1, 0, 2, 3
    )
    produced = produced.reshape(ctx_count, exp_count, per_owner, D)
    returned = lax.all_to_all(
        lax.all_to_all(produced, "ctx", split_axis=0, concat_axis=0, tiled=True),
        "exp",
        split_axis=1,
        concat_axis=1,
        tiled=True,
    )
    inverse = (
        jnp.zeros((length * TOP,), jnp.int32)
        .at[order]
        .set(jnp.arange(length * TOP, dtype=jnp.int32))
    )
    per_route = returned.reshape(length * TOP, D)[inverse].reshape(length, TOP, D)
    combined = jnp.einsum("tj,tjd->td", route_gate[0], per_route.astype(jnp.float32))
    moe_output = combined.astype(jnp.bfloat16)
    return (mixed[None], moe_output[None])


def solution(mesh):
    return jax.shard_map(
        on_device,
        mesh=mesh,
        in_specs=(
            P("exp", "ctx", None),
            P("exp", "ctx", None),
            P("exp", "ctx", None),
            P("exp", "ctx", None),
            P("exp", "ctx", None),
            P("exp", "ctx", None),
            P("exp", "ctx", None),
            P("exp", None, None, None),
            P(),
            P(None, "ctx"),
            P(),
            P("exp", "ctx", None),
            P("exp", "ctx", None),
            P(("ctx", "exp"), None, None),
            P(("ctx", "exp"), None, None),
        ),
        out_specs=(P("exp", "ctx", None), P("exp", "ctx", None)),
        check_vma=False,
    )
```

```python
import functools

import jax
import jax.numpy as jnp
from jax import lax
from jax.experimental import pallas as pl
from jax.experimental.pallas import tpu as pltpu
from jax.sharding import PartitionSpec as P

D = 2048
HK = 8
OUTPUT_CHANNELS = 16
DK = 128
DV = 128
FF = 512
TOP = 10


BF = jnp.bfloat16
MESH = pl.DeviceIdType.MESH
BASE = 16


def mm(a, b):
    return lax.dot_general(
        a.astype(BF), b.astype(BF), (((1,), (0,)), ((), ())), preferred_element_type=jnp.float32
    )


def mm_nt(a, b):
    return lax.dot_general(
        a.astype(BF), b.astype(BF), (((1,), (1,)), ((), ())), preferred_element_type=jnp.float32
    )


def mm_tn(a, b):
    return lax.dot_general(
        a.astype(BF), b.astype(BF), (((0,), (0,)), ((), ())), preferred_element_type=jnp.float32
    )


def unit_lower_inverse(lowers, rows, cols, eye):
    length = rows.shape[0]
    same = (rows // BASE) == (cols // BASE)
    powers = [jnp.where(same, -low, 0.0) for low in lowers]
    xs = [eye + p for p in powers]
    span = 2
    while span < BASE:
        powers = [mm(p, p) for p in powers]
        xs = [x + mm(x, p) for x, p in zip(xs, powers)]
        span *= 2
    size = BASE
    while size < length:
        inside = ((rows // (2 * size)) == (cols // (2 * size))) & ((rows // size) > (cols // size))
        mids = [mm(jnp.where(inside, low, 0.0), x) for low, x in zip(lowers, xs)]
        xs = [x - mm(x, m) for x, m in zip(xs, mids)]
        size *= 2
    return xs


def delta_head(query, keys, values, rate_rows, cum_rows):
    length = query.shape[0]
    rows = lax.broadcasted_iota(jnp.int32, (length, length), 0)
    cols = lax.broadcasted_iota(jnp.int32, (length, length), 1)
    diag = rows == cols
    eye = jnp.where(diag, 1.0, 0.0)
    query = query.astype(jnp.float32)
    key = keys.astype(jnp.float32)
    key = key * lax.rsqrt(jnp.sum(key * key, axis=-1, keepdims=True) + 1e-06)
    kk = mm_nt(key, key)
    qk = mm_nt(query, key)
    column = lambda row: jnp.sum(jnp.where(diag, row, 0.0), axis=1, keepdims=True)
    lowers, parts = [], []
    for value, rate_row, cum_row in zip(values, rate_rows, cum_rows):
        cum, rate = column(cum_row), column(rate_row)
        last = cum_row[:, length - 1 :]
        spread = jnp.exp(jnp.where(rows >= cols, cum - cum_row, 0.0))
        lowers.append(jnp.where(rows > cols, rate * spread * kk, 0.0))
        parts.append((value.astype(jnp.float32), cum, rate, last, spread))
    inverses = unit_lower_inverse(lowers, rows, cols, eye)
    results = []
    for inverse, (value, cum, rate, last, spread) in zip(inverses, parts):
        now = jnp.exp(cum)
        solved = mm(inverse, jnp.concatenate([rate * value, (rate * now) * key], axis=1))
        attend = jnp.where(rows >= cols, spread * qk, 0.0)
        inner = mm(attend, solved)
        tail = mm_tn(jnp.exp(last - cum) * key, solved)
        dv = value.shape[1]
        results.append(
            (
                inner[:, :dv],
                now * query - inner[:, dv:],
                jnp.exp(last) * eye - tail[:, dv:],
                tail[:, :dv],
            )
        )
    return results


def delta_kernel(group, q_ref, k_ref, v_ref, rate_ref, cum_ref, intra_ref, qeff_ref, trans_ref, add_ref):
    width = v_ref.shape[1] // group
    results = delta_head(
        q_ref[...],
        k_ref[...],
        [v_ref[:, i * width : (i + 1) * width] for i in range(group)],
        [rate_ref[0, i : i + 1, :] for i in range(group)],
        [cum_ref[0, i : i + 1, :] for i in range(group)],
    )
    for i, (intra, qeff, trans, add) in enumerate(results):
        intra_ref[i] = intra
        qeff_ref[i] = qeff.astype(qeff_ref.dtype)
        trans_ref[i] = trans.astype(trans_ref.dtype)
        add_ref[i] = add


def delta_local(query, key, value, rate, cum):
    length = query.shape[0]
    heads = rate.shape[0]
    group = heads // HK
    out = jax.ShapeDtypeStruct((heads, length, DV), jnp.float32)
    outb = jax.ShapeDtypeStruct((heads, length, DK), BF)
    sq = jax.ShapeDtypeStruct((heads, DK, DK), BF)
    sv = jax.ShapeDtypeStruct((heads, DK, DV), jnp.float32)
    block = lambda a, b: pl.BlockSpec((group, a, b), lambda h: (h, 0, 0))
    rows = pl.BlockSpec((1, group, length), lambda h: (h, 0, 0))
    return pl.pallas_call(
        functools.partial(delta_kernel, group),
        out_shape=(out, outb, sq, sv),
        grid=(HK,),
        in_specs=[
            pl.BlockSpec((length, DK), lambda h: (0, h)),
            pl.BlockSpec((length, DK), lambda h: (0, h)),
            pl.BlockSpec((length, group * DV), lambda h: (0, h)),
            rows,
            rows,
        ],
        out_specs=(block(length, DV), block(length, DK), block(DK, DK), block(DK, DV)),
        cost_estimate=pl.CostEstimate(flops=20 * heads * 2 * length**3, bytes_accessed=8 << 20, transcendentals=heads * length * length),
    )(query, key, value, rate.reshape(HK, group, length), cum.reshape(HK, group, length))


def mixer_kernel(
    pieces, trans_ref, add_ref, init_ref, intra_ref, qeff_ref, gate_ref, gain_ref, weight_ref, stream_ref, norm_ref,
    mixed_ref, moe_ref, state, leaving, gbuf, rbuf, sbuf,
    state_send, state_recv, g_send, f_send, g_recv, r_send, r_recv,
):
    p = lax.axis_index("ctx")
    n = lax.axis_size("ctx")
    heads, length, dv = intra_ref.shape
    per = heads // pieces
    cols = weight_ref.shape[1]
    core = p % 2
    sibling = p + 1 - 2 * core

    barrier = pltpu.get_barrier_semaphore()
    for d in range(1, n):
        pl.semaphore_signal(barrier, inc=1, device_id={"ctx": (p + d) % n}, device_id_type=MESH)
    pl.semaphore_wait(barrier, n - 1)

    def remote(src, dst, ssem, rsem, device):
        return pltpu.make_async_remote_copy(
            src_ref=src, dst_ref=dst, send_sem=ssem, recv_sem=rsem, device_id={"ctx": device}, device_id_type=MESH
        )

    def state_copy(g):
        return remote(leaving.at[g], state.at[g], state_send.at[g], state_recv.at[g], (p + 1) % n)

    def g_copy(t, g):
        device = sibling if t == 0 else (p + 2 * t) % n
        return remote(gbuf.at[p, g], gbuf.at[p, g], g_send.at[t, g], g_recv.at[p, g], device)

    def forward(q, g):
        return remote(gbuf.at[q, g], gbuf.at[q, g], f_send.at[q, g], g_recv.at[q, g], sibling)

    def r_copy(q):
        return remote(sbuf.at[q], rbuf.at[p], r_send.at[q], r_recv.at[p], q)

    def r_arrival(q):
        return remote(sbuf.at[q], rbuf.at[q], r_send.at[q], r_recv.at[q], q)

    for g in range(pieces):
        @pl.when(p == 0)
        def _():
            state[g] = init_ref[g * per : (g + 1) * per].astype(BF)

        @pl.when(p > 0)
        def _():
            state_copy(g).wait_recv()

        @pl.when(p < n - 1)
        def _():
            for j in range(per):
                h = g * per + j
                leaving[g, j] = (mm(trans_ref[h], state[g, j]) + add_ref[h]).astype(BF)
            state_copy(g).start()

        for j in range(per):
            h = g * per + j
            out = intra_ref[h] + mm(qeff_ref[h], state[g, j])
            out = out * lax.rsqrt(jnp.mean(out * out, axis=-1, keepdims=True) + 1e-06) * gain_ref[...]
            gate = gate_ref[:, h * dv : (h + 1) * dv].astype(jnp.float32)
            gbuf[p, g, :, j * dv : (j + 1) * dv] = (out * (gate / (1.0 + jnp.exp(-gate)))).astype(BF)
        for t in range(n // 2):
            g_copy(t, g).start()

    for q in range(n):
        for g in range(pieces):
            @pl.when(p != q)
            def _():
                forward(q, g).wait_recv()

                @pl.when(p % 2 == q % 2)
                def _():
                    forward(q, g).start()

        block = mm(gbuf[q, 0], weight_ref[0 : per * dv, :])
        for g in range(1, pieces):
            block += mm(gbuf[q, g], weight_ref[g * per * dv : (g + 1) * per * dv, :])

        @pl.when(p == q)
        def _():
            rbuf[q] = block.astype(BF)

        @pl.when(p != q)
        def _():
            sbuf[q] = block.astype(BF)
            r_copy(q).start()

    square = jnp.zeros((length, 1), jnp.float32)
    for q in range(n):
        @pl.when(p != q)
        def _():
            r_arrival(q).wait_recv()

        here = slice(q * cols, (q + 1) * cols)
        mixed = (stream_ref[:, here].astype(jnp.float32) + rbuf[q].astype(jnp.float32)).astype(BF)
        mixed_ref[:, here] = mixed
        mixed = mixed.astype(jnp.float32)
        square += jnp.sum(mixed * mixed, axis=-1, keepdims=True)
    scale = lax.rsqrt(square / (n * cols) + 1e-06)
    for q in range(n):
        here = slice(q * cols, (q + 1) * cols)
        moe_ref[:, here] = (mixed_ref[:, here].astype(jnp.float32) * scale * norm_ref[:, here]).astype(BF)

    for g in range(pieces):
        @pl.when(p < n - 1)
        def _():
            state_copy(g).wait_send()

        for t in range(n // 2):
            g_copy(t, g).wait_send()
    for q in range(n):
        @pl.when(p != q)
        def _():
            r_copy(q).wait_send()

            @pl.when(p % 2 == q % 2)
            def _():
                for g in range(pieces):
                    forward(q, g).wait_send()


def mixer(trans, add, init, intra, qeff, gate, gain, weight, stream, norm):
    heads, length, dv = intra.shape
    n = lax.axis_size("ctx")
    pieces = 4
    per = heads // pieces
    cols = weight.shape[1]
    dma = pltpu.SemaphoreType.DMA
    return pl.pallas_call(
        functools.partial(mixer_kernel, pieces),
        out_shape=(jax.ShapeDtypeStruct(stream.shape, BF), jax.ShapeDtypeStruct(stream.shape, BF)),
        in_specs=[pl.BlockSpec(memory_space=pltpu.VMEM)] * 10,
        out_specs=(pl.BlockSpec(memory_space=pltpu.VMEM), pl.BlockSpec(memory_space=pltpu.VMEM)),
        scratch_shapes=[
            pltpu.VMEM((pieces, per, DK, dv), BF),
            pltpu.VMEM((pieces, per, DK, dv), BF),
            pltpu.VMEM((n, pieces, length, per * dv), BF),
            pltpu.VMEM((n, length, cols), BF),
            pltpu.VMEM((n, length, cols), BF),
            dma((pieces,)), dma((pieces,)),
            dma((n // 2, pieces)), dma((n, pieces)), dma((n, pieces)),
            dma((n,)), dma((n,)),
        ],
        compiler_params=pltpu.CompilerParams(collective_id=2, has_side_effects=True),
    )(trans, add, init, intra, qeff, gate, gain.reshape(1, -1), weight, stream, norm.reshape(1, -1))


def moe_kernel(
    planes, lanes_x, tok_ref, pick_ref, up_ref, down_ref, out_ref,
    tokbuf, pickbuf, sendbuf, recvbuf, prodbuf, retbuf, partbuf, zbuf, total,
    tok_send, tok_recv, pick_send, pick_recv, d_send, d_recv, r_send, r_recv, z_send, z_recv,
):
    c = lax.axis_index("ctx")
    e = lax.axis_index("exp")
    z = e // lanes_x
    x = e % lanes_x
    ctx = lax.axis_size("ctx")
    peers = ctx * lanes_x
    mine = c * lanes_x + x
    slots = sendbuf.shape[2]
    width = tok_ref.shape[1]
    ff = down_ref.shape[0]

    def plane_device(q):
        return (q // lanes_x, z * lanes_x + q % lanes_x)

    def line_device(zz):
        return (c, zz * lanes_x + x)

    barrier = pltpu.get_barrier_semaphore()
    for d in range(1, peers):
        pl.semaphore_signal(barrier, inc=1, device_id=plane_device((mine + d) % peers), device_id_type=MESH)
    for d in range(1, planes):
        pl.semaphore_signal(barrier, inc=1, device_id=line_device((z + d) % planes), device_id_type=MESH)
    pl.semaphore_wait(barrier, peers + planes - 2)

    def remote(src, dst, ssem, rsem, device):
        return pltpu.make_async_remote_copy(
            src_ref=src, dst_ref=dst, send_sem=ssem, recv_sem=rsem, device_id=device, device_id_type=MESH
        )

    def step_of(i):
        return (i % 2) * ((i + 1) // 2) + (1 - i % 2) * ((planes - i // 2) % planes)

    def tok_copy(s):
        return remote(tok_ref, tokbuf.at[s], tok_send.at[s], tok_recv.at[s], line_device((z + s) % planes))

    def pick_copy(s):
        there = (z + s) % planes
        return remote(pick_ref.at[there], pickbuf.at[s], pick_send.at[s], pick_recv.at[s], line_device(there))

    def d_copy(s, q):
        return remote(sendbuf.at[s, q], recvbuf.at[s, mine], d_send.at[s, q], d_recv.at[s, mine], plane_device(q))

    def d_arrival(s, q):
        return remote(sendbuf.at[s, q], recvbuf.at[s, q], d_send.at[s, q], d_recv.at[s, q], plane_device(q))

    def r_copy(s, q):
        return remote(prodbuf.at[s, q], retbuf.at[s, mine], r_send.at[s, q], r_recv.at[s, mine], plane_device(q))

    def r_arrival(s, q):
        return remote(prodbuf.at[s, q], retbuf.at[s, q], r_send.at[s, q], r_recv.at[s, q], plane_device(q))

    def z_copy(s):
        return remote(partbuf.at[s], zbuf.at[s], z_send.at[s], z_recv.at[s], line_device((z - s + planes) % planes))

    for i in range(1, planes):
        s = (i + 1) // 2 if i % 2 else (planes - i // 2) % planes
        pick_copy(s).start()
        tok_copy(s).start()
    tokbuf[0] = tok_ref[...]
    pickbuf[0] = pick_ref[z]

    def body(i, carry):
        @pl.when(i < planes)
        def _():
            s = step_of(i)

            @pl.when(i > 0)
            def _():
                pick_copy(s).wait_recv()
                tok_copy(s).wait_recv()

            chosen = jnp.where(pickbuf[s].astype(jnp.float32) != 0.0, 1.0, 0.0).astype(BF)
            rows = mm(chosen, tokbuf[s])
            sendbuf[s] = rows.reshape(peers, slots, width).astype(BF)
            for d in range(1, peers):
                d_copy(s, (mine + d) % peers).start()
            recvbuf[s, mine] = sendbuf[s, mine]

        @pl.when((i >= 1) & (i < planes + 1))
        def _():
            s = step_of(i - 1)
            for d in range(1, peers):
                d_arrival(s, (mine + d) % peers).wait_recv()
            rows = recvbuf[s].astype(jnp.float32).reshape(peers * slots, width).astype(BF)
            gate = mm(rows, up_ref[:, :ff])
            hidden = (gate / (1.0 + jnp.exp(-gate)) * mm(rows, up_ref[:, ff:])).astype(BF)
            made = mm(hidden, down_ref[...])
            prodbuf[s] = made.reshape(peers, slots, width).astype(BF)
            for d in range(1, peers):
                r_copy(s, (mine + d) % peers).start()
            retbuf[s, mine] = prodbuf[s, mine]

        @pl.when(i >= 2)
        def _():
            s = step_of(i - 2)
            for d in range(1, peers):
                r_arrival(s, (mine + d) % peers).wait_recv()
            rows = retbuf[s].astype(jnp.float32).reshape(peers * slots, width).astype(BF)
            part = mm_tn(pickbuf[s], rows)

            @pl.when(i == 2)
            def _():
                total[...] = part

            @pl.when(i > 2)
            def _():
                partbuf[s] = part.astype(BF)
                z_copy(s).start()

        return carry

    lax.fori_loop(0, planes + 2, body, 0)

    for s in range(1, planes):
        z_copy(s).wait_recv()
        total[...] += zbuf[s].astype(jnp.float32)
    out_ref[...] = total[...].astype(out_ref.dtype)

    for s in range(1, planes):
        tok_copy(s).wait_send()
        pick_copy(s).wait_send()
        z_copy(s).wait_send()

    def drain(s, carry):
        for d in range(1, peers):
            d_copy(s, (mine + d) % peers).wait_send()
            r_copy(s, (mine + d) % peers).wait_send()
        return carry

    lax.fori_loop(0, planes, drain, 0)


def moe_planes(moe_in, routes, route_gate, expert_up, expert_down, planes, lanes_x):
    length, width = moe_in.shape
    ctx = lax.axis_size("ctx")
    peers = ctx * lanes_x
    experts = peers * planes
    slots = length * TOP // experts
    ids = jnp.arange(experts, dtype=jnp.int32)
    hit = routes[:, :, None] == ids
    named = jnp.any(hit, axis=1)
    weight = jnp.sum(jnp.where(hit, route_gate[:, :, None], 0.0), axis=1).T
    ones = named.astype(BF)
    before = (
        lax.broadcasted_iota(jnp.int32, (length, length), 0)
        < lax.broadcasted_iota(jnp.int32, (length, length), 1)
    ).astype(BF)
    rank = lax.dot_general(ones, before, (((0,), (0,)), ((), ())), preferred_element_type=jnp.float32)
    rank = jnp.where(named.T, rank, -1.0)

    def by_plane(v):
        return v.reshape(ctx, planes, lanes_x, length).transpose(1, 0, 2, 3)

    slot = jnp.arange(slots, dtype=jnp.float32)[None, None, None, :, None]
    pick = jnp.where(by_plane(rank)[:, :, :, None, :] == slot, by_plane(weight)[:, :, :, None, :], 0.0)
    pick = pick.astype(BF).reshape(planes, peers * slots, length)
    dma = pltpu.SemaphoreType.DMA
    rows_shape = pltpu.VMEM((planes, peers, slots, width), BF)
    block = pltpu.VMEM((planes, length, width), BF)
    return pl.pallas_call(
        functools.partial(moe_kernel, planes, lanes_x),
        out_shape=jax.ShapeDtypeStruct((length, width), BF),
        in_specs=[pl.BlockSpec(memory_space=pltpu.VMEM)] * 4,
        out_specs=pl.BlockSpec(memory_space=pltpu.VMEM),
        scratch_shapes=[
            block,
            pltpu.VMEM((planes, peers * slots, length), BF),
            rows_shape, rows_shape, rows_shape, rows_shape,
            block,
            block,
            pltpu.VMEM((length, width), jnp.float32),
            dma((planes,)), dma((planes,)), dma((planes,)), dma((planes,)),
            dma((planes, peers)), dma((planes, peers)), dma((planes, peers)), dma((planes, peers)),
            dma((planes,)), dma((planes,)),
        ],
        compiler_params=pltpu.CompilerParams(collective_id=1, has_side_effects=True, vmem_limit_bytes=60 << 20),
    )(moe_in, pick, expert_up[0], expert_down[0])


def on_device(
    stream,
    queries,
    key_proj,
    value_proj,
    gate_proj,
    write_rate,
    log_decay,
    init_state,
    head_gain,
    out_weight,
    moe_gain,
    routes,
    route_gate,
    expert_up,
    expert_down,
):
    length = stream.shape[1]
    cumulative = jnp.cumsum(log_decay[0], axis=0).T
    intra, query_eff, transit, carry_add = delta_local(
        queries[0], key_proj[0], value_proj[0], write_rate[0].T, cumulative
    )
    mixed, moe_in = mixer(
        transit, carry_add, init_state[0], intra, query_eff, gate_proj[0], head_gain, out_weight, stream[0], moe_gain
    )
    ctx_count = lax.axis_size("ctx")
    exp_count = lax.axis_size("exp")
    local_experts = expert_up.shape[0]
    lanes_x = max(1, ctx_count // 2)
    even = exp_count % lanes_x == 0 and length * TOP % (8 * ctx_count * exp_count) == 0
    if local_experts == 1 and even:
        moe_output = moe_planes(
            moe_in, routes[0], route_gate[0], expert_up, expert_down, exp_count // lanes_x, lanes_x
        )
        return (mixed[None], moe_output[None])
    flat_routes = routes[0].reshape(-1)
    order = jnp.argsort(flat_routes, stable=True)
    per_owner = length * TOP // (ctx_count * exp_count)
    outgoing = moe_in[order // TOP].reshape(ctx_count, exp_count, per_owner, D)
    arrived = lax.all_to_all(
        lax.all_to_all(outgoing, "ctx", split_axis=0, concat_axis=0, tiled=True),
        "exp",
        split_axis=1,
        concat_axis=1,
        tiled=True,
    )
    slot_count = per_owner // local_experts
    grouped = arrived.reshape(ctx_count * exp_count, local_experts, slot_count, D).transpose(
        1, 0, 2, 3
    )
    grouped = grouped.reshape(local_experts, ctx_count * exp_count * slot_count, D)
    pre = jnp.einsum("erd,edf->erf", grouped, expert_up, preferred_element_type=jnp.float32)
    hidden = (jax.nn.silu(pre[:, :, :FF]) * pre[:, :, FF:]).astype(jnp.bfloat16)
    produced = jnp.einsum(
        "erf,efd->erd", hidden, expert_down, preferred_element_type=jnp.float32
    ).astype(jnp.bfloat16)
    produced = produced.reshape(local_experts, ctx_count * exp_count, slot_count, D).transpose(
        1, 0, 2, 3
    )
    produced = produced.reshape(ctx_count, exp_count, per_owner, D)
    returned = lax.all_to_all(
        lax.all_to_all(produced, "ctx", split_axis=0, concat_axis=0, tiled=True),
        "exp",
        split_axis=1,
        concat_axis=1,
        tiled=True,
    )
    inverse = (
        jnp.zeros((length * TOP,), jnp.int32)
        .at[order]
        .set(jnp.arange(length * TOP, dtype=jnp.int32))
    )
    per_route = returned.reshape(length * TOP, D)[inverse].reshape(length, TOP, D)
    combined = jnp.einsum("tj,tjd->td", route_gate[0], per_route.astype(jnp.float32))
    moe_output = combined.astype(jnp.bfloat16)
    return (mixed[None], moe_output[None])


def solution(mesh):
    return jax.shard_map(
        on_device,
        mesh=mesh,
        in_specs=(
            P("exp", "ctx", None),
            P("exp", "ctx", None),
            P("exp", "ctx", None),
            P("exp", "ctx", None),
            P("exp", "ctx", None),
            P("exp", "ctx", None),
            P("exp", "ctx", None),
            P("exp", None, None, None),
            P(),
            P(None, "ctx"),
            P(),
            P("exp", "ctx", None),
            P("exp", "ctx", None),
            P(("ctx", "exp"), None, None),
            P(("ctx", "exp"), None, None),
        ),
        out_specs=(P("exp", "ctx", None), P("exp", "ctx", None)),
        check_vma=False,
    )
```

```python
import functools

import jax
import jax.numpy as jnp
from jax import lax
from jax.experimental import pallas as pl
from jax.experimental.pallas import tpu as pltpu
from jax.sharding import PartitionSpec as P

D = 2048
HK = 8
OUTPUT_CHANNELS = 16
DK = 128
DV = 128
FF = 512
TOP = 10


BF = jnp.bfloat16
MESH = pl.DeviceIdType.MESH
BASE = 16


def mm(a, b):
    return lax.dot_general(
        a.astype(BF), b.astype(BF), (((1,), (0,)), ((), ())), preferred_element_type=jnp.float32
    )


def mm_nt(a, b):
    return lax.dot_general(
        a.astype(BF), b.astype(BF), (((1,), (1,)), ((), ())), preferred_element_type=jnp.float32
    )


def mm_tn(a, b):
    return lax.dot_general(
        a.astype(BF), b.astype(BF), (((0,), (0,)), ((), ())), preferred_element_type=jnp.float32
    )


def unit_lower_inverse(lowers, rows, cols, eye):
    length = rows.shape[0]
    same = (rows // BASE) == (cols // BASE)
    powers = [jnp.where(same, -low, 0.0) for low in lowers]
    xs = [eye + p for p in powers]
    span = 2
    while span < BASE:
        powers = [mm(p, p) for p in powers]
        xs = [x + mm(x, p) for x, p in zip(xs, powers)]
        span *= 2
    size = BASE
    while size < length:
        inside = ((rows // (2 * size)) == (cols // (2 * size))) & ((rows // size) > (cols // size))
        mids = [mm(jnp.where(inside, low, 0.0), x) for low, x in zip(lowers, xs)]
        xs = [x - mm(x, m) for x, m in zip(xs, mids)]
        size *= 2
    return xs


def delta_heads(queries, keys, values, rate_rows, cum_rows):
    length = queries[0].shape[0]
    group = len(values) // len(queries)
    rows = lax.broadcasted_iota(jnp.int32, (length, length), 0)
    cols = lax.broadcasted_iota(jnp.int32, (length, length), 1)
    diag = rows == cols
    eye = jnp.where(diag, 1.0, 0.0)
    units, scores, overlaps = [], [], []
    for query, key in zip(queries, keys):
        key = key.astype(jnp.float32)
        key = key * lax.rsqrt(jnp.sum(key * key, axis=-1, keepdims=True) + 1e-06)
        units.append(key)
        overlaps.append(mm_nt(key, key))
        scores.append(mm_nt(query, key))
    column = lambda row: jnp.sum(jnp.where(diag, row, 0.0), axis=1, keepdims=True)
    lowers, parts = [], []
    for i, (value, rate_row, cum_row) in enumerate(zip(values, rate_rows, cum_rows)):
        cum, rate = column(cum_row), column(rate_row)
        last = cum_row[:, length - 1 :]
        spread = jnp.exp(jnp.where(rows >= cols, cum - cum_row, 0.0))
        lowers.append(jnp.where(rows > cols, rate * spread * overlaps[i // group], 0.0))
        attend = jnp.where(rows >= cols, spread * scores[i // group], 0.0)
        parts.append((value.astype(jnp.float32), cum, rate, last, attend))
    inverses = unit_lower_inverse(lowers, rows, cols, eye)
    results = []
    for i, (inverse, (value, cum, rate, last, attend)) in enumerate(zip(inverses, parts)):
        key, query = units[i // group], queries[i // group].astype(jnp.float32)
        now = jnp.exp(cum)
        solved = mm(inverse, jnp.concatenate([rate * value, (rate * now) * key], axis=1))
        inner = mm(attend, solved)
        tail = mm_tn(jnp.exp(last - cum) * key, solved)
        dv = value.shape[1]
        results.append(
            (
                inner[:, :dv],
                now * query - inner[:, dv:],
                jnp.exp(last) * eye - tail[:, dv:],
                tail[:, :dv],
            )
        )
    return results


def mixer_kernel(
    pieces, query_ref, key_ref, value_ref, rate_ref, cum_ref, init_ref, gate_ref, gain_ref, weight_hbm, stream_ref,
    norm_ref, mixed_ref, moe_ref, state, leaving, gbuf, rbuf, sbuf, weight_ref, weight_sem, state_send, state_recv, g_send, f_send, g_recv, r_send, r_recv,
):
    p = lax.axis_index("ctx")
    n = lax.axis_size("ctx")
    heads, dv = init_ref.shape[0], init_ref.shape[2]
    length = query_ref.shape[0]
    per = heads // pieces
    shared = HK // pieces
    cols = weight_ref.shape[1]
    fetch = pltpu.make_async_copy(weight_hbm, weight_ref, weight_sem)
    fetch.start()
    core = p % 2
    sibling = p + 1 - 2 * core

    barrier = pltpu.get_barrier_semaphore()
    for d in range(1, n):
        pl.semaphore_signal(barrier, inc=1, device_id={"ctx": (p + d) % n}, device_id_type=MESH)
    pl.semaphore_wait(barrier, n - 1)

    def remote(src, dst, ssem, rsem, device):
        return pltpu.make_async_remote_copy(
            src_ref=src, dst_ref=dst, send_sem=ssem, recv_sem=rsem, device_id={"ctx": device}, device_id_type=MESH
        )

    def state_copy(g):
        return remote(leaving.at[g], state.at[g], state_send.at[g], state_recv.at[g], (p + 1) % n)

    def g_copy(t, g):
        device = sibling if t == 0 else (p + 2 * t) % n
        return remote(gbuf.at[p, g], gbuf.at[p, g], g_send.at[t, g], g_recv.at[p, g], device)

    def forward(q, g):
        return remote(gbuf.at[q, g], gbuf.at[q, g], f_send.at[q, g], g_recv.at[q, g], sibling)

    def r_copy(q):
        return remote(sbuf.at[q], rbuf.at[p], r_send.at[q], r_recv.at[p], q)

    def r_arrival(q):
        return remote(sbuf.at[q], rbuf.at[q], r_send.at[q], r_recv.at[q], q)

    def piece(g, carry):
        qcols = [pl.ds(pl.multiple_of((g * shared + j) * DK, DK), DK) for j in range(shared)]
        vcols = [pl.ds(pl.multiple_of((g * per + j) * dv, dv), dv) for j in range(per)]
        results = delta_heads(
            [query_ref[:, c] for c in qcols],
            [key_ref[:, c] for c in qcols],
            [value_ref[:, c] for c in vcols],
            [rate_ref[g, j : j + 1, :] for j in range(per)],
            [cum_ref[g, j : j + 1, :] for j in range(per)],
        )

        @pl.when(p == 0)
        def _():
            for j in range(per):
                state[g, j] = init_ref[g * per + j].astype(BF)

        @pl.when(p > 0)
        def _():
            state_copy(g).wait_recv()

        @pl.when(p < n - 1)
        def _():
            for j in range(per):
                leaving[g, j] = (mm(results[j][2], state[g, j]) + results[j][3]).astype(BF)
            state_copy(g).start()

        for j in range(per):
            out = results[j][0] + mm(results[j][1], state[g, j])
            out = out * lax.rsqrt(jnp.mean(out * out, axis=-1, keepdims=True) + 1e-06) * gain_ref[...]
            gate = gate_ref[:, vcols[j]].astype(jnp.float32)
            gbuf[p, g, :, j * dv : (j + 1) * dv] = (out * (gate / (1.0 + jnp.exp(-gate)))).astype(BF)
        for t in range(n // 2):
            g_copy(t, g).start()
        return carry

    lax.fori_loop(0, pieces, piece, 0)
    fetch.wait()

    for q in range(n):
        for g in range(pieces):
            @pl.when(p != q)
            def _():
                forward(q, g).wait_recv()

                @pl.when(p % 2 == q % 2)
                def _():
                    forward(q, g).start()

        block = mm(gbuf[q, 0], weight_ref[0 : per * dv, :])
        for g in range(1, pieces):
            block += mm(gbuf[q, g], weight_ref[g * per * dv : (g + 1) * per * dv, :])

        @pl.when(p == q)
        def _():
            rbuf[q] = block.astype(BF)

        @pl.when(p != q)
        def _():
            sbuf[q] = block.astype(BF)
            r_copy(q).start()

    square = jnp.zeros((length, 1), jnp.float32)
    for q in range(n):
        @pl.when(p != q)
        def _():
            r_arrival(q).wait_recv()

        here = slice(q * cols, (q + 1) * cols)
        mixed = (stream_ref[:, here].astype(jnp.float32) + rbuf[q].astype(jnp.float32)).astype(BF)
        mixed_ref[:, here] = mixed
        mixed = mixed.astype(jnp.float32)
        square += jnp.sum(mixed * mixed, axis=-1, keepdims=True)
    scale = lax.rsqrt(square / (n * cols) + 1e-06)
    for q in range(n):
        here = slice(q * cols, (q + 1) * cols)
        moe_ref[:, here] = (mixed_ref[:, here].astype(jnp.float32) * scale * norm_ref[:, here]).astype(BF)

    for g in range(pieces):
        @pl.when(p < n - 1)
        def _():
            state_copy(g).wait_send()

        for t in range(n // 2):
            g_copy(t, g).wait_send()
    for q in range(n):
        @pl.when(p != q)
        def _():
            r_copy(q).wait_send()

            @pl.when(p % 2 == q % 2)
            def _():
                for g in range(pieces):
                    forward(q, g).wait_send()


def mixer(query, key, value, rate, cum, init, gate, gain, weight, stream, norm):
    heads, _, dv = init.shape
    length = query.shape[0]
    n = lax.axis_size("ctx")
    pieces = HK // 2
    per = heads // pieces
    cols = weight.shape[1]
    dma = pltpu.SemaphoreType.DMA
    vmem = pl.BlockSpec(memory_space=pltpu.VMEM)
    return pl.pallas_call(
        functools.partial(mixer_kernel, pieces),
        out_shape=(jax.ShapeDtypeStruct(stream.shape, BF), jax.ShapeDtypeStruct(stream.shape, BF)),
        in_specs=[vmem] * 8 + [pl.BlockSpec(memory_space=pl.ANY)] + [vmem] * 2,
        out_specs=(vmem, vmem),
        scratch_shapes=[
            pltpu.VMEM((pieces, per, DK, dv), BF),
            pltpu.VMEM((pieces, per, DK, dv), BF),
            pltpu.VMEM((n, pieces, length, per * dv), BF),
            pltpu.VMEM((n, length, cols), BF),
            pltpu.VMEM((n, length, cols), BF),
            pltpu.VMEM(weight.shape, BF),
            dma(()),
            dma((pieces,)), dma((pieces,)),
            dma((n // 2, pieces)), dma((n, pieces)), dma((n, pieces)),
            dma((n,)), dma((n,)),
        ],
        compiler_params=pltpu.CompilerParams(collective_id=2, has_side_effects=True),
    )(
        query, key, value, rate.reshape(pieces, per, length), cum.reshape(pieces, per, length), init, gate,
        gain.reshape(1, -1), weight, stream, norm.reshape(1, -1),
    )


def moe_kernel(
    planes, lanes_x, tok_ref, pick_ref, up_hbm, down_hbm, out_ref,
    up_ref, down_ref, w_sem, tokbuf, pickbuf, sendbuf, recvbuf, prodbuf, retbuf, partbuf, zbuf, total,
    tok_send, tok_recv, pick_send, pick_recv, d_send, d_recv, r_send, r_recv, z_send, z_recv,
):
    c = lax.axis_index("ctx")
    e = lax.axis_index("exp")
    z = e // lanes_x
    x = e % lanes_x
    ctx = lax.axis_size("ctx")
    peers = ctx * lanes_x
    mine = c * lanes_x + x
    slots = sendbuf.shape[2]
    width = tok_ref.shape[1]
    ff = down_ref.shape[0]
    fetches = (
        pltpu.make_async_copy(up_hbm, up_ref, w_sem.at[0]),
        pltpu.make_async_copy(down_hbm, down_ref, w_sem.at[1]),
    )
    for fetch in fetches:
        fetch.start()

    def plane_device(q):
        return (q // lanes_x, z * lanes_x + q % lanes_x)

    def line_device(zz):
        return (c, zz * lanes_x + x)

    barrier = pltpu.get_barrier_semaphore()
    for d in range(1, peers):
        pl.semaphore_signal(barrier, inc=1, device_id=plane_device((mine + d) % peers), device_id_type=MESH)
    for d in range(1, planes):
        pl.semaphore_signal(barrier, inc=1, device_id=line_device((z + d) % planes), device_id_type=MESH)
    pl.semaphore_wait(barrier, peers + planes - 2)

    def remote(src, dst, ssem, rsem, device):
        return pltpu.make_async_remote_copy(
            src_ref=src, dst_ref=dst, send_sem=ssem, recv_sem=rsem, device_id=device, device_id_type=MESH
        )

    def step_of(i):
        return (i % 2) * ((i + 1) // 2) + (1 - i % 2) * ((planes - i // 2) % planes)

    def tok_copy(s):
        return remote(tok_ref, tokbuf.at[s], tok_send.at[s], tok_recv.at[s], line_device((z + s) % planes))

    def pick_copy(s):
        there = (z + s) % planes
        return remote(pick_ref.at[there], pickbuf.at[s], pick_send.at[s], pick_recv.at[s], line_device(there))

    def d_copy(s, q):
        return remote(sendbuf.at[s, q], recvbuf.at[s, mine], d_send.at[s, q], d_recv.at[s, mine], plane_device(q))

    def d_arrival(s, q):
        return remote(sendbuf.at[s, q], recvbuf.at[s, q], d_send.at[s, q], d_recv.at[s, q], plane_device(q))

    def r_copy(s, q):
        return remote(prodbuf.at[s, q], retbuf.at[s, mine], r_send.at[s, q], r_recv.at[s, mine], plane_device(q))

    def r_arrival(s, q):
        return remote(prodbuf.at[s, q], retbuf.at[s, q], r_send.at[s, q], r_recv.at[s, q], plane_device(q))

    def z_copy(s):
        return remote(partbuf.at[s], zbuf.at[s], z_send.at[s], z_recv.at[s], line_device((z - s + planes) % planes))

    for i in range(1, planes):
        s = (i + 1) // 2 if i % 2 else (planes - i // 2) % planes
        pick_copy(s).start()
        tok_copy(s).start()
    tokbuf[0] = tok_ref[...]
    pickbuf[0] = pick_ref[z]

    def body(i, carry):
        @pl.when(i < planes)
        def _():
            s = step_of(i)

            @pl.when(i > 0)
            def _():
                pick_copy(s).wait_recv()
                tok_copy(s).wait_recv()

            chosen = jnp.where(pickbuf[s].astype(jnp.float32) != 0.0, 1.0, 0.0).astype(BF)
            rows = mm(chosen, tokbuf[s])
            sendbuf[s] = rows.reshape(peers, slots, width).astype(BF)
            for d in range(1, peers):
                d_copy(s, (mine + d) % peers).start()
            recvbuf[s, mine] = sendbuf[s, mine]

        @pl.when(i == 2)
        def _():
            for fetch in fetches:
                fetch.wait()

        @pl.when((i >= 2) & (i < planes + 2))
        def _():
            s = step_of((i - 1) % planes)
            for d in range(1, peers):
                d_arrival(s, (mine + d) % peers).wait_recv()
            rows = recvbuf[s].astype(jnp.float32).reshape(peers * slots, width).astype(BF)
            gate = mm(rows, up_ref[:, :ff])
            hidden = (gate / (1.0 + jnp.exp(-gate)) * mm(rows, up_ref[:, ff:])).astype(BF)
            made = mm(hidden, down_ref[...])
            prodbuf[s] = made.reshape(peers, slots, width).astype(BF)
            for d in range(1, peers):
                r_copy(s, (mine + d) % peers).start()
            retbuf[s, mine] = prodbuf[s, mine]

        @pl.when(i >= 3)
        def _():
            s = step_of((i - 2) % planes)
            for d in range(1, peers):
                r_arrival(s, (mine + d) % peers).wait_recv()
            rows = retbuf[s].astype(jnp.float32).reshape(peers * slots, width).astype(BF)
            part = mm_tn(pickbuf[s], rows)

            @pl.when(i == planes + 2)
            def _():
                total[...] = part

            @pl.when(i < planes + 2)
            def _():
                partbuf[s] = part.astype(BF)
                z_copy(s).start()

        return carry

    lax.fori_loop(0, planes + 3, body, 0)

    for s in range(1, planes):
        z_copy(s).wait_recv()
        total[...] += zbuf[s].astype(jnp.float32)
    out_ref[...] = total[...].astype(out_ref.dtype)

    for s in range(1, planes):
        tok_copy(s).wait_send()
        pick_copy(s).wait_send()
        z_copy(s).wait_send()

    def drain(s, carry):
        for d in range(1, peers):
            d_copy(s, (mine + d) % peers).wait_send()
            r_copy(s, (mine + d) % peers).wait_send()
        return carry

    lax.fori_loop(0, planes, drain, 0)


def moe_planes(moe_in, routes, route_gate, expert_up, expert_down, planes, lanes_x):
    length, width = moe_in.shape
    ctx = lax.axis_size("ctx")
    peers = ctx * lanes_x
    experts = peers * planes
    slots = length * TOP // experts
    ids = jnp.arange(experts, dtype=jnp.int32)
    hit = routes[:, :, None] == ids
    named = jnp.any(hit, axis=1)
    weight = jnp.sum(jnp.where(hit, route_gate[:, :, None], 0.0), axis=1).T
    ones = named.astype(BF)
    before = (
        lax.broadcasted_iota(jnp.int32, (length, length), 0)
        < lax.broadcasted_iota(jnp.int32, (length, length), 1)
    ).astype(BF)
    rank = lax.dot_general(ones, before, (((0,), (0,)), ((), ())), preferred_element_type=jnp.float32)
    rank = jnp.where(named.T, rank, -1.0)

    def by_plane(v):
        return v.reshape(ctx, planes, lanes_x, length).transpose(1, 0, 2, 3)

    slot = jnp.arange(slots, dtype=jnp.float32)[None, None, None, :, None]
    pick = jnp.where(by_plane(rank)[:, :, :, None, :] == slot, by_plane(weight)[:, :, :, None, :], 0.0)
    pick = pick.astype(BF).reshape(planes, peers * slots, length)
    dma = pltpu.SemaphoreType.DMA
    rows_shape = pltpu.VMEM((planes, peers, slots, width), BF)
    block = pltpu.VMEM((planes, length, width), BF)
    return pl.pallas_call(
        functools.partial(moe_kernel, planes, lanes_x),
        out_shape=jax.ShapeDtypeStruct((length, width), BF),
        in_specs=[pl.BlockSpec(memory_space=pltpu.VMEM)] * 2 + [pl.BlockSpec(memory_space=pl.ANY)] * 2,
        out_specs=pl.BlockSpec(memory_space=pltpu.VMEM),
        scratch_shapes=[
            pltpu.VMEM(expert_up.shape[1:], BF),
            pltpu.VMEM(expert_down.shape[1:], BF),
            dma((2,)),
            block,
            pltpu.VMEM((planes, peers * slots, length), BF),
            rows_shape, rows_shape, rows_shape, rows_shape,
            block,
            block,
            pltpu.VMEM((length, width), jnp.float32),
            dma((planes,)), dma((planes,)), dma((planes,)), dma((planes,)),
            dma((planes, peers)), dma((planes, peers)), dma((planes, peers)), dma((planes, peers)),
            dma((planes,)), dma((planes,)),
        ],
        compiler_params=pltpu.CompilerParams(collective_id=1, has_side_effects=True, vmem_limit_bytes=60 << 20),
    )(moe_in, pick, expert_up[0], expert_down[0])


def on_device(
    stream,
    queries,
    key_proj,
    value_proj,
    gate_proj,
    write_rate,
    log_decay,
    init_state,
    head_gain,
    out_weight,
    moe_gain,
    routes,
    route_gate,
    expert_up,
    expert_down,
):
    length = stream.shape[1]
    cumulative = jnp.cumsum(log_decay[0], axis=0).T
    mixed, moe_in = mixer(
        queries[0], key_proj[0], value_proj[0], write_rate[0].T, cumulative, init_state[0], gate_proj[0],
        head_gain, out_weight, stream[0], moe_gain,
    )
    ctx_count = lax.axis_size("ctx")
    exp_count = lax.axis_size("exp")
    local_experts = expert_up.shape[0]
    lanes_x = max(1, ctx_count // 2)
    even = exp_count % lanes_x == 0 and length * TOP % (8 * ctx_count * exp_count) == 0
    if local_experts == 1 and even:
        moe_output = moe_planes(
            moe_in, routes[0], route_gate[0], expert_up, expert_down, exp_count // lanes_x, lanes_x
        )
        return (mixed[None], moe_output[None])
    flat_routes = routes[0].reshape(-1)
    order = jnp.argsort(flat_routes, stable=True)
    per_owner = length * TOP // (ctx_count * exp_count)
    outgoing = moe_in[order // TOP].reshape(ctx_count, exp_count, per_owner, D)
    arrived = lax.all_to_all(
        lax.all_to_all(outgoing, "ctx", split_axis=0, concat_axis=0, tiled=True),
        "exp",
        split_axis=1,
        concat_axis=1,
        tiled=True,
    )
    slot_count = per_owner // local_experts
    grouped = arrived.reshape(ctx_count * exp_count, local_experts, slot_count, D).transpose(
        1, 0, 2, 3
    )
    grouped = grouped.reshape(local_experts, ctx_count * exp_count * slot_count, D)
    pre = jnp.einsum("erd,edf->erf", grouped, expert_up, preferred_element_type=jnp.float32)
    hidden = (jax.nn.silu(pre[:, :, :FF]) * pre[:, :, FF:]).astype(jnp.bfloat16)
    produced = jnp.einsum(
        "erf,efd->erd", hidden, expert_down, preferred_element_type=jnp.float32
    ).astype(jnp.bfloat16)
    produced = produced.reshape(local_experts, ctx_count * exp_count, slot_count, D).transpose(
        1, 0, 2, 3
    )
    produced = produced.reshape(ctx_count, exp_count, per_owner, D)
    returned = lax.all_to_all(
        lax.all_to_all(produced, "ctx", split_axis=0, concat_axis=0, tiled=True),
        "exp",
        split_axis=1,
        concat_axis=1,
        tiled=True,
    )
    inverse = (
        jnp.zeros((length * TOP,), jnp.int32)
        .at[order]
        .set(jnp.arange(length * TOP, dtype=jnp.int32))
    )
    per_route = returned.reshape(length * TOP, D)[inverse].reshape(length, TOP, D)
    combined = jnp.einsum("tj,tjd->td", route_gate[0], per_route.astype(jnp.float32))
    moe_output = combined.astype(jnp.bfloat16)
    return (mixed[None], moe_output[None])


def solution(mesh):
    return jax.shard_map(
        on_device,
        mesh=mesh,
        in_specs=(
            P("exp", "ctx", None),
            P("exp", "ctx", None),
            P("exp", "ctx", None),
            P("exp", "ctx", None),
            P("exp", "ctx", None),
            P("exp", "ctx", None),
            P("exp", "ctx", None),
            P("exp", None, None, None),
            P(),
            P(None, "ctx"),
            P(),
            P("exp", "ctx", None),
            P("exp", "ctx", None),
            P(("ctx", "exp"), None, None),
            P(("ctx", "exp"), None, None),
        ),
        out_specs=(P("exp", "ctx", None), P("exp", "ctx", None)),
        check_vma=False,
    )
```

```python
import functools

import jax
import jax.numpy as jnp
from jax import lax
from jax.experimental import pallas as pl
from jax.experimental.pallas import tpu as pltpu
from jax.sharding import PartitionSpec as P

D = 2048
HK = 8
OUTPUT_CHANNELS = 16
DK = 128
DV = 128
FF = 512
TOP = 10


BF = jnp.bfloat16
MESH = pl.DeviceIdType.MESH
BASE = 16


def mm(a, b):
    return lax.dot_general(
        a.astype(BF), b.astype(BF), (((1,), (0,)), ((), ())), preferred_element_type=jnp.float32
    )


def mm_nt(a, b):
    return lax.dot_general(
        a.astype(BF), b.astype(BF), (((1,), (1,)), ((), ())), preferred_element_type=jnp.float32
    )


def mm_tn(a, b):
    return lax.dot_general(
        a.astype(BF), b.astype(BF), (((0,), (0,)), ((), ())), preferred_element_type=jnp.float32
    )


def unit_lower_inverse(lowers, rows, cols, eye):
    length = rows.shape[0]
    same = (rows // BASE) == (cols // BASE)
    powers = [jnp.where(same, -low, 0.0) for low in lowers]
    xs = [eye + p for p in powers]
    span = 2
    while span < BASE:
        powers = [mm(p, p) for p in powers]
        xs = [x + mm(x, p) for x, p in zip(xs, powers)]
        span *= 2
    size = BASE
    while size < length:
        inside = ((rows // (2 * size)) == (cols // (2 * size))) & ((rows // size) > (cols // size))
        mids = [mm(jnp.where(inside, low, 0.0), x) for low, x in zip(lowers, xs)]
        xs = [x - mm(x, m) for x, m in zip(xs, mids)]
        size *= 2
    return xs


def delta_heads(queries, keys, values, rate_rows, cum_rows):
    length = queries[0].shape[0]
    group = len(values) // len(queries)
    rows = lax.broadcasted_iota(jnp.int32, (length, length), 0)
    cols = lax.broadcasted_iota(jnp.int32, (length, length), 1)
    diag = rows == cols
    eye = jnp.where(diag, 1.0, 0.0)
    units, scores, overlaps = [], [], []
    for query, key in zip(queries, keys):
        key = key.astype(jnp.float32)
        key = key * lax.rsqrt(jnp.sum(key * key, axis=-1, keepdims=True) + 1e-06)
        units.append(key)
        overlaps.append(mm_nt(key, key))
        scores.append(mm_nt(query, key))
    column = lambda row: jnp.sum(jnp.where(diag, row, 0.0), axis=1, keepdims=True)
    lowers, parts = [], []
    for i, (value, rate_row, cum_row) in enumerate(zip(values, rate_rows, cum_rows)):
        cum, rate = column(cum_row), column(rate_row)
        last = cum_row[:, length - 1 :]
        spread = jnp.exp(jnp.where(rows >= cols, cum - cum_row, 0.0))
        lowers.append(jnp.where(rows > cols, rate * spread * overlaps[i // group], 0.0))
        attend = jnp.where(rows >= cols, spread * scores[i // group], 0.0)
        parts.append((value.astype(jnp.float32), cum, rate, last, attend))
    inverses = unit_lower_inverse(lowers, rows, cols, eye)
    results = []
    for i, (inverse, (value, cum, rate, last, attend)) in enumerate(zip(inverses, parts)):
        key, query = units[i // group], queries[i // group].astype(jnp.float32)
        now = jnp.exp(cum)
        solved = mm(inverse, jnp.concatenate([rate * value, (rate * now) * key], axis=1))
        inner = mm(attend, solved)
        tail = mm_tn(jnp.exp(last - cum) * key, solved)
        dv = value.shape[1]
        results.append(
            (
                inner[:, :dv],
                now * query - inner[:, dv:],
                jnp.exp(last) * eye - tail[:, dv:],
                tail[:, :dv],
            )
        )
    return results


def mixer_kernel(
    pieces, query_ref, key_ref, value_ref, rate_ref, cum_ref, init_ref, gate_ref, gain_ref, weight_hbm, stream_ref,
    norm_ref, mixed_ref, moe_ref, state, leaving, gbuf, rbuf, sbuf, weight_ref, weight_sem, state_send, state_recv, g_send, f_send, g_recv, r_send, r_recv,
):
    p = lax.axis_index("ctx")
    n = lax.axis_size("ctx")
    heads, dv = init_ref.shape[0], init_ref.shape[2]
    length = query_ref.shape[0]
    per = heads // pieces
    shared = HK // pieces
    cols = weight_ref.shape[1]
    fetch = pltpu.make_async_copy(weight_hbm, weight_ref, weight_sem)
    fetch.start()
    core = p % 2
    sibling = p + 1 - 2 * core

    barrier = pltpu.get_barrier_semaphore()
    for d in range(1, n):
        pl.semaphore_signal(barrier, inc=1, device_id={"ctx": (p + d) % n}, device_id_type=MESH)
    pl.semaphore_wait(barrier, n - 1)

    def remote(src, dst, ssem, rsem, device):
        return pltpu.make_async_remote_copy(
            src_ref=src, dst_ref=dst, send_sem=ssem, recv_sem=rsem, device_id={"ctx": device}, device_id_type=MESH
        )

    def state_copy(g):
        return remote(leaving.at[g], state.at[g], state_send.at[g], state_recv.at[g], (p + 1) % n)

    def g_copy(t, g):
        device = sibling if t == 0 else (p + 2 * t) % n
        return remote(gbuf.at[p, g], gbuf.at[p, g], g_send.at[t, g], g_recv.at[p, g], device)

    def forward(q, g):
        return remote(gbuf.at[q, g], gbuf.at[q, g], f_send.at[q, g], g_recv.at[q, g], sibling)

    def r_copy(q):
        return remote(sbuf.at[q], rbuf.at[p], r_send.at[q], r_recv.at[p], q)

    def r_arrival(q):
        return remote(sbuf.at[q], rbuf.at[q], r_send.at[q], r_recv.at[q], q)

    def piece(g, carry):
        qcols = [pl.ds(pl.multiple_of((g * shared + j) * DK, DK), DK) for j in range(shared)]
        vcols = [pl.ds(pl.multiple_of((g * per + j) * dv, dv), dv) for j in range(per)]
        results = delta_heads(
            [query_ref[:, c] for c in qcols],
            [key_ref[:, c] for c in qcols],
            [value_ref[:, c] for c in vcols],
            [rate_ref[g, j : j + 1, :] for j in range(per)],
            [cum_ref[g, j : j + 1, :] for j in range(per)],
        )

        @pl.when(p == 0)
        def _():
            for j in range(per):
                state[g, j] = init_ref[g * per + j].astype(BF)

        @pl.when(p > 0)
        def _():
            state_copy(g).wait_recv()

        @pl.when(p < n - 1)
        def _():
            for j in range(per):
                leaving[g, j] = (mm(results[j][2], state[g, j]) + results[j][3]).astype(BF)
            state_copy(g).start()

        for j in range(per):
            out = results[j][0] + mm(results[j][1], state[g, j])
            out = out * lax.rsqrt(jnp.mean(out * out, axis=-1, keepdims=True) + 1e-06) * gain_ref[...]
            gate = gate_ref[:, vcols[j]].astype(jnp.float32)
            gbuf[p, g, :, j * dv : (j + 1) * dv] = (out * (gate / (1.0 + jnp.exp(-gate)))).astype(BF)
        for t in range(n // 2):
            g_copy(t, g).start()
        return carry

    lax.fori_loop(0, pieces, piece, 0)
    fetch.wait()

    for q in range(n):
        for g in range(pieces):
            @pl.when(p != q)
            def _():
                forward(q, g).wait_recv()

                @pl.when(p % 2 == q % 2)
                def _():
                    forward(q, g).start()

        block = mm(gbuf[q, 0], weight_ref[0 : per * dv, :])
        for g in range(1, pieces):
            block += mm(gbuf[q, g], weight_ref[g * per * dv : (g + 1) * per * dv, :])

        @pl.when(p == q)
        def _():
            rbuf[q] = block.astype(BF)

        @pl.when(p != q)
        def _():
            sbuf[q] = block.astype(BF)
            r_copy(q).start()

    square = jnp.zeros((length, 1), jnp.float32)
    for q in range(n):
        @pl.when(p != q)
        def _():
            r_arrival(q).wait_recv()

        here = slice(q * cols, (q + 1) * cols)
        mixed = (stream_ref[:, here].astype(jnp.float32) + rbuf[q].astype(jnp.float32)).astype(BF)
        mixed_ref[:, here] = mixed
        mixed = mixed.astype(jnp.float32)
        square += jnp.sum(mixed * mixed, axis=-1, keepdims=True)
    scale = lax.rsqrt(square / (n * cols) + 1e-06)
    for q in range(n):
        here = slice(q * cols, (q + 1) * cols)
        moe_ref[:, here] = (mixed_ref[:, here].astype(jnp.float32) * scale * norm_ref[:, here]).astype(BF)

    for g in range(pieces):
        @pl.when(p < n - 1)
        def _():
            state_copy(g).wait_send()

        for t in range(n // 2):
            g_copy(t, g).wait_send()
    for q in range(n):
        @pl.when(p != q)
        def _():
            r_copy(q).wait_send()

            @pl.when(p % 2 == q % 2)
            def _():
                for g in range(pieces):
                    forward(q, g).wait_send()


def mixer(query, key, value, rate, cum, init, gate, gain, weight, stream, norm):
    heads, _, dv = init.shape
    length = query.shape[0]
    n = lax.axis_size("ctx")
    pieces = HK // 2
    per = heads // pieces
    cols = weight.shape[1]
    dma = pltpu.SemaphoreType.DMA
    vmem = pl.BlockSpec(memory_space=pltpu.VMEM)
    return pl.pallas_call(
        functools.partial(mixer_kernel, pieces),
        out_shape=(jax.ShapeDtypeStruct(stream.shape, BF), jax.ShapeDtypeStruct(stream.shape, BF)),
        in_specs=[vmem] * 8 + [pl.BlockSpec(memory_space=pl.ANY)] + [vmem] * 2,
        out_specs=(vmem, vmem),
        scratch_shapes=[
            pltpu.VMEM((pieces, per, DK, dv), BF),
            pltpu.VMEM((pieces, per, DK, dv), BF),
            pltpu.VMEM((n, pieces, length, per * dv), BF),
            pltpu.VMEM((n, length, cols), BF),
            pltpu.VMEM((n, length, cols), BF),
            pltpu.VMEM(weight.shape, BF),
            dma(()),
            dma((pieces,)), dma((pieces,)),
            dma((n // 2, pieces)), dma((n, pieces)), dma((n, pieces)),
            dma((n,)), dma((n,)),
        ],
        compiler_params=pltpu.CompilerParams(collective_id=2, has_side_effects=True),
    )(
        query, key, value, rate.reshape(pieces, per, length), cum.reshape(pieces, per, length), init, gate,
        gain.reshape(1, -1), weight, stream, norm.reshape(1, -1),
    )


def moe_kernel(
    planes, lanes_x, tok_ref, pick_ref, up_hbm, down_hbm, out_ref,
    up_ref, down_ref, w_sem, tokbuf, pickbuf, sendbuf, recvbuf, prodbuf, retbuf, partbuf, zbuf, total,
    own_send, tok_send, tok_recv, pick_send, pick_recv, d_send, d_recv, r_send, r_recv, z_send, z_recv,
):
    c = lax.axis_index("ctx")
    e = lax.axis_index("exp")
    z = e // lanes_x
    x = e % lanes_x
    ctx = lax.axis_size("ctx")
    peers = ctx * lanes_x
    mine = c * lanes_x + x
    slots = sendbuf.shape[2]
    width = tok_ref.shape[1]
    ff = down_ref.shape[0]
    fetches = (
        pltpu.make_async_copy(up_hbm, up_ref, w_sem.at[0]),
        pltpu.make_async_copy(down_hbm, down_ref, w_sem.at[1]),
    )
    for fetch in fetches:
        fetch.start()

    def plane_device(q):
        return (q // lanes_x, z * lanes_x + q % lanes_x)

    def line_device(zz):
        return (c, zz * lanes_x + x)

    barrier = pltpu.get_barrier_semaphore()
    for d in range(1, peers):
        pl.semaphore_signal(barrier, inc=1, device_id=plane_device((mine + d) % peers), device_id_type=MESH)
    for d in range(1, planes):
        pl.semaphore_signal(barrier, inc=1, device_id=line_device((z + d) % planes), device_id_type=MESH)
    pl.semaphore_wait(barrier, peers + planes - 2)

    def remote(src, dst, ssem, rsem, device):
        return pltpu.make_async_remote_copy(
            src_ref=src, dst_ref=dst, send_sem=ssem, recv_sem=rsem, device_id=device, device_id_type=MESH
        )

    fewer = jnp.where(2 * z < planes, z, planes - 1 - z)

    def place(k):
        paired = k <= 2 * fewer
        distance = jnp.where(paired, (k + 1) // 2, k - fewer)
        lower = jnp.where(paired, k % 2 == 1, 2 * z >= planes)
        return lower, jnp.where(k == 0, 0, jnp.where(lower, distance, planes - distance))

    def step_of(k):
        return place(k)[1]

    def tok_up(s):
        return remote(tokbuf.at[s], tokbuf.at[s + 1], tok_send.at[s], tok_recv.at[s + 1], line_device((z + 1) % planes))

    def tok_down(s):
        return remote(
            tokbuf.at[s], tokbuf.at[s - 1], tok_send.at[s], tok_recv.at[s - 1], line_device((z + planes - 1) % planes)
        )

    own_up = remote(tok_ref, tokbuf.at[1], own_send.at[0], tok_recv.at[1], line_device((z + 1) % planes))
    own_down = remote(
        tok_ref, tokbuf.at[planes - 1], own_send.at[1], tok_recv.at[planes - 1],
        line_device((z + planes - 1) % planes),
    )

    def pick_copy(s):
        there = (z + s) % planes
        return remote(pick_ref.at[there], pickbuf.at[s], pick_send.at[s], pick_recv.at[s], line_device(there))

    def d_copy(s, q):
        return remote(sendbuf.at[s, q], recvbuf.at[s, mine], d_send.at[s, q], d_recv.at[s, mine], plane_device(q))

    def d_arrival(s, q):
        return remote(sendbuf.at[s, q], recvbuf.at[s, q], d_send.at[s, q], d_recv.at[s, q], plane_device(q))

    def r_copy(s, q):
        return remote(prodbuf.at[s, q], retbuf.at[s, mine], r_send.at[s, q], r_recv.at[s, mine], plane_device(q))

    def r_arrival(s, q):
        return remote(prodbuf.at[s, q], retbuf.at[s, q], r_send.at[s, q], r_recv.at[s, q], plane_device(q))

    def z_copy(s):
        return remote(partbuf.at[s], zbuf.at[s], z_send.at[s], z_recv.at[s], line_device((z - s + planes) % planes))

    @pl.when(z + 1 < planes)
    def _():
        own_up.start()

    @pl.when(z > 0)
    def _():
        own_down.start()

    for s in range(1, planes):
        pick_copy(s).start()
    tokbuf[0] = tok_ref[...]
    pickbuf[0] = pick_ref[z]

    def body(i, carry):
        @pl.when(i < planes)
        def _():
            s = step_of(i)

            @pl.when(i > 0)
            def _():
                lower = place(i)[0]
                tok_up(s - 1).wait_recv()

                @pl.when(lower & (z + 1 < planes))
                def _():
                    tok_up(s).start()

                @pl.when(jnp.logical_not(lower) & (z > 0))
                def _():
                    tok_down(s).start()

                pick_copy(s).wait_recv()

            chosen = jnp.where(pickbuf[s].astype(jnp.float32) != 0.0, 1.0, 0.0).astype(BF)
            rows = mm(chosen, tokbuf[s])
            sendbuf[s] = rows.reshape(peers, slots, width).astype(BF)
            for d in range(1, peers):
                d_copy(s, (mine + d) % peers).start()
            recvbuf[s, mine] = sendbuf[s, mine]

        @pl.when(i == 2)
        def _():
            for fetch in fetches:
                fetch.wait()

        @pl.when((i >= 2) & (i < planes + 2))
        def _():
            s = step_of((i - 1) % planes)
            for d in range(1, peers):
                d_arrival(s, (mine + d) % peers).wait_recv()
            rows = recvbuf[s].astype(jnp.float32).reshape(peers * slots, width).astype(BF)
            gate = mm(rows, up_ref[:, :ff])
            hidden = (gate / (1.0 + jnp.exp(-gate)) * mm(rows, up_ref[:, ff:])).astype(BF)
            made = mm(hidden, down_ref[...])
            prodbuf[s] = made.reshape(peers, slots, width).astype(BF)
            for d in range(1, peers):
                r_copy(s, (mine + d) % peers).start()
            retbuf[s, mine] = prodbuf[s, mine]

        @pl.when(i >= 3)
        def _():
            s = step_of((i - 2) % planes)
            for d in range(1, peers):
                r_arrival(s, (mine + d) % peers).wait_recv()
            rows = retbuf[s].astype(jnp.float32).reshape(peers * slots, width).astype(BF)
            part = mm_tn(pickbuf[s], rows)

            @pl.when(i == planes + 2)
            def _():
                total[...] = part

            @pl.when(i < planes + 2)
            def _():
                partbuf[s] = part.astype(BF)
                z_copy(s).start()

        return carry

    lax.fori_loop(0, planes + 3, body, 0)

    for s in range(1, planes):
        z_copy(s).wait_recv()
        total[...] += zbuf[s].astype(jnp.float32)
    out_ref[...] = total[...].astype(out_ref.dtype)

    @pl.when(z + 1 < planes)
    def _():
        own_up.wait_send()

    @pl.when(z > 0)
    def _():
        own_down.wait_send()

    for s in range(1, planes):
        @pl.when((s <= z) & (z + 1 < planes))
        def _():
            tok_up(s).wait_send()

        @pl.when((s > z) & (z > 0))
        def _():
            tok_down(s).wait_send()

        pick_copy(s).wait_send()
        z_copy(s).wait_send()

    def drain(s, carry):
        for d in range(1, peers):
            d_copy(s, (mine + d) % peers).wait_send()
            r_copy(s, (mine + d) % peers).wait_send()
        return carry

    lax.fori_loop(0, planes, drain, 0)


def moe_planes(moe_in, routes, route_gate, expert_up, expert_down, planes, lanes_x):
    length, width = moe_in.shape
    ctx = lax.axis_size("ctx")
    peers = ctx * lanes_x
    experts = peers * planes
    slots = length * TOP // experts
    ids = jnp.arange(experts, dtype=jnp.int32)
    hit = routes[:, :, None] == ids
    named = jnp.any(hit, axis=1)
    weight = jnp.sum(jnp.where(hit, route_gate[:, :, None], 0.0), axis=1).T
    ones = named.astype(BF)
    before = (
        lax.broadcasted_iota(jnp.int32, (length, length), 0)
        < lax.broadcasted_iota(jnp.int32, (length, length), 1)
    ).astype(BF)
    rank = lax.dot_general(ones, before, (((0,), (0,)), ((), ())), preferred_element_type=jnp.float32)
    rank = jnp.where(named.T, rank, -1.0)

    def by_plane(v):
        return v.reshape(ctx, planes, lanes_x, length).transpose(1, 0, 2, 3)

    slot = jnp.arange(slots, dtype=jnp.float32)[None, None, None, :, None]
    pick = jnp.where(by_plane(rank)[:, :, :, None, :] == slot, by_plane(weight)[:, :, :, None, :], 0.0)
    pick = pick.astype(BF).reshape(planes, peers * slots, length)
    dma = pltpu.SemaphoreType.DMA
    rows_shape = pltpu.VMEM((planes, peers, slots, width), BF)
    block = pltpu.VMEM((planes, length, width), BF)
    return pl.pallas_call(
        functools.partial(moe_kernel, planes, lanes_x),
        out_shape=jax.ShapeDtypeStruct((length, width), BF),
        in_specs=[pl.BlockSpec(memory_space=pltpu.VMEM)] * 2 + [pl.BlockSpec(memory_space=pl.ANY)] * 2,
        out_specs=pl.BlockSpec(memory_space=pltpu.VMEM),
        scratch_shapes=[
            pltpu.VMEM(expert_up.shape[1:], BF),
            pltpu.VMEM(expert_down.shape[1:], BF),
            dma((2,)),
            block,
            pltpu.VMEM((planes, peers * slots, length), BF),
            rows_shape, rows_shape, rows_shape, rows_shape,
            block,
            block,
            pltpu.VMEM((length, width), jnp.float32),
            dma((2,)), dma((planes,)), dma((planes,)), dma((planes,)), dma((planes,)),
            dma((planes, peers)), dma((planes, peers)), dma((planes, peers)), dma((planes, peers)),
            dma((planes,)), dma((planes,)),
        ],
        compiler_params=pltpu.CompilerParams(collective_id=1, has_side_effects=True, vmem_limit_bytes=60 << 20),
    )(moe_in, pick, expert_up[0], expert_down[0])


def on_device(
    stream,
    queries,
    key_proj,
    value_proj,
    gate_proj,
    write_rate,
    log_decay,
    init_state,
    head_gain,
    out_weight,
    moe_gain,
    routes,
    route_gate,
    expert_up,
    expert_down,
):
    length = stream.shape[1]
    cumulative = jnp.cumsum(log_decay[0], axis=0).T
    mixed, moe_in = mixer(
        queries[0], key_proj[0], value_proj[0], write_rate[0].T, cumulative, init_state[0], gate_proj[0],
        head_gain, out_weight, stream[0], moe_gain,
    )
    ctx_count = lax.axis_size("ctx")
    exp_count = lax.axis_size("exp")
    local_experts = expert_up.shape[0]
    lanes_x = max(1, ctx_count // 2)
    even = exp_count % lanes_x == 0 and length * TOP % (8 * ctx_count * exp_count) == 0
    if local_experts == 1 and even:
        moe_output = moe_planes(
            moe_in, routes[0], route_gate[0], expert_up, expert_down, exp_count // lanes_x, lanes_x
        )
        return (mixed[None], moe_output[None])
    flat_routes = routes[0].reshape(-1)
    order = jnp.argsort(flat_routes, stable=True)
    per_owner = length * TOP // (ctx_count * exp_count)
    outgoing = moe_in[order // TOP].reshape(ctx_count, exp_count, per_owner, D)
    arrived = lax.all_to_all(
        lax.all_to_all(outgoing, "ctx", split_axis=0, concat_axis=0, tiled=True),
        "exp",
        split_axis=1,
        concat_axis=1,
        tiled=True,
    )
    slot_count = per_owner // local_experts
    grouped = arrived.reshape(ctx_count * exp_count, local_experts, slot_count, D).transpose(
        1, 0, 2, 3
    )
    grouped = grouped.reshape(local_experts, ctx_count * exp_count * slot_count, D)
    pre = jnp.einsum("erd,edf->erf", grouped, expert_up, preferred_element_type=jnp.float32)
    hidden = (jax.nn.silu(pre[:, :, :FF]) * pre[:, :, FF:]).astype(jnp.bfloat16)
    produced = jnp.einsum(
        "erf,efd->erd", hidden, expert_down, preferred_element_type=jnp.float32
    ).astype(jnp.bfloat16)
    produced = produced.reshape(local_experts, ctx_count * exp_count, slot_count, D).transpose(
        1, 0, 2, 3
    )
    produced = produced.reshape(ctx_count, exp_count, per_owner, D)
    returned = lax.all_to_all(
        lax.all_to_all(produced, "ctx", split_axis=0, concat_axis=0, tiled=True),
        "exp",
        split_axis=1,
        concat_axis=1,
        tiled=True,
    )
    inverse = (
        jnp.zeros((length * TOP,), jnp.int32)
        .at[order]
        .set(jnp.arange(length * TOP, dtype=jnp.int32))
    )
    per_route = returned.reshape(length * TOP, D)[inverse].reshape(length, TOP, D)
    combined = jnp.einsum("tj,tjd->td", route_gate[0], per_route.astype(jnp.float32))
    moe_output = combined.astype(jnp.bfloat16)
    return (mixed[None], moe_output[None])


def solution(mesh):
    return jax.shard_map(
        on_device,
        mesh=mesh,
        in_specs=(
            P("exp", "ctx", None),
            P("exp", "ctx", None),
            P("exp", "ctx", None),
            P("exp", "ctx", None),
            P("exp", "ctx", None),
            P("exp", "ctx", None),
            P("exp", "ctx", None),
            P("exp", None, None, None),
            P(),
            P(None, "ctx"),
            P(),
            P("exp", "ctx", None),
            P("exp", "ctx", None),
            P(("ctx", "exp"), None, None),
            P(("ctx", "exp"), None, None),
        ),
        out_specs=(P("exp", "ctx", None), P("exp", "ctx", None)),
        check_vma=False,
    )
```
